256 devices in a mesh: dp: 32 (over y, z), rows: 8 (over x, core).
Axes of the slice: x: 4, y: 4, z: 8, core: 2. Of those that a mesh axis runs over, the one named last changes fastest.
Arguments:
- real_frames: bfloat16 [32, 3, 128, 256], P('dp', None, 'rows'), may hold values from -4 to 4
- fake_frames: bfloat16 [32, 3, 128, 256], P('dp', None, 'rows'), may hold values from -4 to 4
- conv_one: bfloat16 [3, 3, 3, 64], replicated, may hold values from -1.25 to 1.25
- conv_two: bfloat16 [3, 3, 64, 128], replicated, may hold values from -0.25 to 0.25
- conv_three: bfloat16 [3, 3, 128, 256], replicated, may hold values from -0.1875 to 0.1875
- conv_four: bfloat16 [3, 3, 256, 512], replicated, may hold values from -0.125 to 0.125
- conv_five: bfloat16 [3, 3, 512, 512], replicated, may hold values from -0.09375 to 0.09375
- bias_one: float32 [64], replicated, may hold values from -2 to 2
- bias_two: float32 [128], replicated, may hold values from -2 to 2
- bias_three: float32 [256], replicated, may hold values from -2 to 2
- bias_four: float32 [512], replicated, may hold values from -2 to 2
- bias_five: float32 [512], replicated, may hold values from -2 to 2
- linear_one: float32 [64], replicated, may hold values from 0.05 to 2
- linear_two: float32 [128], replicated, may hold values from 0.05 to 2
- linear_three: float32 [256], replicated, may hold values from 0.05 to 2
- linear_four: float32 [512], replicated, may hold values from 0.05 to 2
- linear_five: float32 [512], replicated, may hold values from 0.25 to 10
Outputs:
- tap_losses: float32 [5], replicated
- fake_grad: float32 [32, 3, 128, 256], P('dp', None, 'rows')
The draws below stay inside these ranges and needn't reach their ends.
All inputs are finite; a program needn't handle non-finite values.
Results may differ from the reference program's by a relative error of at most 0.0065.
Values may be sent and summed in bfloat16 or wider, within the bound.
A program may use at most 128 MiB of HBM per device.

```python
import math
import jax
import jax.numpy as jnp
from jax import lax

C1 = 64
C2 = 128
C3 = 256
C4 = 512
C5 = 512
WIDTH = 256
FRAMES = 32
HEIGHT = 128


def coarse_field(key):
    small = jax.random.normal(key, (FRAMES, 3, HEIGHT // 16, WIDTH // 16), jnp.float32)
    return jnp.repeat(jnp.repeat(small, 16, axis=2), 16, axis=3)


def frame_pair(key):
    base = jax.random.fold_in(key, 4711)
    keys = jax.random.split(base, 4)
    rough_real = jax.random.normal(keys[0], (FRAMES, 3, HEIGHT, WIDTH), jnp.float32)
    rough_diff = jax.random.normal(keys[1], (FRAMES, 3, HEIGHT, WIDTH), jnp.float32)
    coarse_real = coarse_field(keys[2])
    coarse_diff = coarse_field(keys[3])
    place = jnp.arange(FRAMES, dtype=jnp.float32) / max(FRAMES - 1, 1)
    rise = 0.3 + 0.7 * place
    real = 0.5 * rough_real + 0.8 * coarse_real
    fake = real + rise[:, None, None, None] * (0.4 * rough_diff + 0.8 * coarse_diff)
    return (jnp.clip(real, -4.0, 4.0), jnp.clip(fake, -4.0, 4.0))


def draw_real_frames(key, part):
    return frame_pair(key)[0].astype(jnp.bfloat16)


def draw_fake_frames(key, part):
    return frame_pair(key)[1].astype(jnp.bfloat16)


def noise(own_key, dims, spread, reach, kind=jnp.bfloat16):
    array = spread * jax.random.normal(own_key, dims, jnp.float32)
    return jnp.clip(array, min=-reach, max=reach).astype(kind)


def setup_inputs(seed: int = 0) -> dict:
    key_of = jax.random.split(jax.random.key(seed), 18)
    real_frames = draw_real_frames(jax.random.fold_in(key_of[17], 71), 0)
    fake_frames = draw_fake_frames(jax.random.fold_in(key_of[17], 71), 0)
    conv_one = noise(key_of[2], (3, 3, 3, C1), 27 ** -0.5, 1.25)
    conv_two = noise(key_of[3], (3, 3, C1, C2), (9 * C1) ** -0.5, 0.25)
    conv_three = noise(key_of[4], (3, 3, C2, C3), (9 * C2) ** -0.5, 0.1875)
    conv_four = noise(key_of[5], (3, 3, C3, C4), (9 * C3) ** -0.5, 0.125)
    conv_five = noise(key_of[6], (3, 3, C4, C5), (9 * C4) ** -0.5, 0.09375)
    bias_one = noise(key_of[7], (C1,), 0.5, 2.0, jnp.float32)
    bias_two = noise(key_of[8], (C2,), 0.5, 2.0, jnp.float32)
    bias_three = noise(key_of[9], (C3,), 0.5, 2.0, jnp.float32)
    bias_four = noise(key_of[10], (C4,), 0.5, 2.0, jnp.float32)
    bias_five = noise(key_of[11], (C5,), 0.5, 2.0, jnp.float32)
    linear_one = jnp.clip(jnp.exp(jax.random.uniform(key_of[12], (C1,), jnp.float32, math.log(0.05), math.log(2.0))), 0.05, 2.0)
    linear_two = jnp.clip(jnp.exp(jax.random.uniform(key_of[13], (C2,), jnp.float32, math.log(0.05), math.log(2.0))), 0.05, 2.0)
    linear_three = jnp.clip(jnp.exp(jax.random.uniform(key_of[14], (C3,), jnp.float32, math.log(0.05), math.log(2.0))), 0.05, 2.0)
    linear_four = jnp.clip(jnp.exp(jax.random.uniform(key_of[15], (C4,), jnp.float32, math.log(0.05), math.log(2.0))), 0.05, 2.0)
    linear_five = jnp.clip(jnp.exp(jax.random.uniform(key_of[16], (C5,), jnp.float32, math.log(0.25), math.log(10.0))), 0.25, 10.0)
    return {"real_frames": real_frames, "fake_frames": fake_frames, "conv_one": conv_one, "conv_two": conv_two, "conv_three": conv_three, "conv_four": conv_four, "conv_five": conv_five, "bias_one": bias_one, "bias_two": bias_two, "bias_three": bias_three, "bias_four": bias_four, "bias_five": bias_five, "linear_one": linear_one, "linear_two": linear_two, "linear_three": linear_three, "linear_four": linear_four, "linear_five": linear_five}


EPS = 1e-06

def smooth(values):
    return jax.nn.gelu(values, approximate=True)

def smooth_back(pre_act, grad_out):
    _, pullback = jax.vjp(smooth, pre_act)
    return pullback(grad_out)[0]

def conv_same(inputs, kernel):
    return lax.conv_general_dilated(inputs.astype(jnp.float32), kernel.astype(jnp.float32), (1, 1), ((1, 1), (1, 1)), dimension_numbers=('NHWC', 'HWIO', 'NHWC'), precision=lax.Precision.HIGHEST)

def flipped(kernel):
    return jnp.transpose(jnp.flip(kernel, (0, 1)), (0, 1, 3, 2))

def pool_half(values):
    shaped = values.astype(jnp.float32).reshape(values.shape[0], values.shape[1] // 2, 2, values.shape[2] // 2, 2, values.shape[3])
    return lax.optimization_barrier(jnp.mean(shaped, axis=(2, 4))).astype(jnp.bfloat16)

def unpool_half(values):
    return jnp.repeat(jnp.repeat(values, 2, axis=1), 2, axis=2) * 0.25

def tap_terms(real_feat, fake_feat, linear):
    real_float = real_feat.astype(jnp.float32)
    fake_float = fake_feat.astype(jnp.float32)
    real_norm = jnp.sqrt(lax.optimization_barrier(jnp.sum(real_float * real_float, axis=-1, keepdims=True)) + EPS)
    fake_norm = jnp.sqrt(lax.optimization_barrier(jnp.sum(fake_float * fake_float, axis=-1, keepdims=True)) + EPS)
    real_unit = real_float / real_norm
    fake_unit = fake_float / fake_norm
    differ = real_unit - fake_unit
    tap_map = lax.optimization_barrier(jnp.sum(linear * differ * differ, axis=-1))
    upward = -2.0 * linear * differ
    tap_grad = (upward - fake_unit * lax.optimization_barrier(jnp.sum(fake_unit * upward, axis=-1, keepdims=True))) / fake_norm
    return (tap_map, tap_grad)

def one_frame(pair, kernels, biases, linears):
    real_frame, fake_frame = pair
    inputs = jnp.transpose(jnp.stack([real_frame, fake_frame]), (0, 2, 3, 1))
    stored = []
    values = []
    for segment_no in range(5):
        pre_act = conv_same(inputs, kernels[segment_no]) + biases[segment_no]
        post_act = smooth(pre_act).astype(jnp.bfloat16)
        tap_map, tap_grad = tap_terms(post_act[0:1], post_act[1:2], linears[segment_no])
        values.append(jnp.mean(tap_map))
        stored.append((pre_act[1:2], tap_grad))
        if segment_no < 4:
            inputs = pool_half(post_act)
    grad_input = None
    for segment_no in range(4, -1, -1):
        pre_fake, tap_grad = stored[segment_no]
        grad_act = tap_grad * 4.0 ** segment_no
        if grad_input is not None:
            grad_act = grad_act + unpool_half(grad_input)
        grad_pre = smooth_back(pre_fake, grad_act).astype(jnp.bfloat16)
        grad_input = conv_same(grad_pre, flipped(kernels[segment_no]))
    return (jnp.stack(values), jnp.transpose(grad_input[0], (2, 0, 1)))

def reference(real_frames, fake_frames, conv_one, conv_two, conv_three, conv_four, conv_five, bias_one, bias_two, bias_three, bias_four, bias_five, linear_one, linear_two, linear_three, linear_four, linear_five):
    kernels = (conv_one, conv_two, conv_three, conv_four, conv_five)
    biases = (bias_one, bias_two, bias_three, bias_four, bias_five)
    linears = (linear_one, linear_two, linear_three, linear_four, linear_five)

    def per_frame(pair):
        return one_frame(pair, kernels, biases, linears)
    values, grads = lax.map(per_frame, (real_frames, fake_frames))
    return (lax.optimization_barrier(jnp.mean(values, axis=0)), grads)
```

```python
import functools

import jax
import jax.numpy as jnp
from jax import lax
from jax.experimental import pallas as pl
from jax.experimental.pallas import tpu as pltpu
from jax.sharding import PartitionSpec as P

MESH = pl.DeviceIdType.MESH
F32 = jnp.float32
BF = jnp.bfloat16
EPS = 1e-06
ROOT = 0.7978845608028654
CUBE = 0.044715

ROWS = 8
NZ = 8
NY = 4


def dot(a, b):
    return lax.dot_general(a, b, (((1,), (0,)), ((), ())), preferred_element_type=F32)


def dot_t(a, b):
    return lax.dot_general(a, b, (((1,), (1,)), ((), ())), preferred_element_type=F32)


def iota(shape, dim):
    return lax.broadcasted_iota(jnp.int32, shape, dim)


def onehot(cond):
    return jnp.where(cond, 1.0, 0.0).astype(BF)


def rounded(x):
    return x.astype(BF).astype(F32)


def gelu(x):
    t = jnp.tanh(x * (ROOT + (ROOT * CUBE) * (x * x)))
    return x * (0.5 + 0.5 * t)


def gelu_both(x):
    x2 = x * x
    t = jnp.tanh(x * (ROOT + (ROOT * CUBE) * x2))
    h = 0.5 + 0.5 * t
    slope = h + (0.5 * x) * (1.0 - t * t) * (ROOT + (3.0 * ROOT * CUBE) * x2)
    return x * h, slope


def tap(r, f, lin, total):
    a = lax.rsqrt(total(r * r) + EPS)
    b = lax.rsqrt(total(f * f) + EPS)
    nf = f * b
    d = r * a - nf
    ld = lin * d
    grad = (ld - nf * total(nf * ld)) * (-2.0 * b)
    return ld * d, grad


def lane_sum(x):
    return jnp.sum(x, axis=-1, keepdims=True)


def fold(x):
    m, c = x.shape
    y = jnp.sum(x.reshape(m // 8, 8, c), axis=0)
    out = y[:, 0:128]
    for j in range(1, c // 128):
        out = out + y[:, j * 128 : (j + 1) * 128]
    return out


def shifted(v, phases):
    c = v.shape[-1]
    q = iota((16, c), 0)
    n = phases * 16
    tail = jnp.where(q < 15, pltpu.roll(v[0:16], 15, 0), 0.0)
    head = jnp.where(q > 0, pltpu.roll(v[n - 16 : n], 1, 0), 0.0)
    if phases == 1:
        return head, tail
    left = jnp.concatenate([head, v[0 : n - 16]], axis=0)
    right = jnp.concatenate([v[16:n], tail], axis=0)
    return left, right


def pool_cols(v, phases):
    c = v.shape[-1]
    return jnp.sum(v.reshape(phases // 2, 2, 16, c), axis=1).reshape(phases * 8, c)


def spread_cols(v, phases):
    c = v.shape[-1]
    y = jnp.broadcast_to(v.reshape(phases, 1, 16, c), (phases, 2, 16, c))
    return y.reshape(phases * 32, c)


def body(
    real_ref, fake_ref, w1_ref, w2_hbm, w3_hbm, w4_hbm, w5_hbm,
    b1_ref, b2_ref, b3_ref, b4_ref, b5_ref, l1_ref, l2_ref, l3_ref, l4_ref, l5_ref,
    loss_ref, grad_ref,
    w2s, w2t, w3s, w4s, w5s, wsm, wb, vec, tt,
    x2, x3, x4, x5, g2, g3, g4, g5, gp1,
    a1, s1, a2, s2, a3, s3, a4, s4,
    stage0, land0, stage2, land2, stage3, land3, stage4, land4, land5, stage5,
    bs4, bl4, bs3, bl3, bs2, bl2, bs1, bl1,
    parts, own, lrow, lz, ly,
    wsem, ssem, rsem, gsend, grecv, lsend, lrecv,
):
    dp = lax.axis_index("dp")
    me = lax.axis_index("rows")
    zi = lax.rem(dp, NZ)
    yi = lax.div(dp, NZ)

    def row_peer(k):
        return (dp, lax.rem(me + k, ROWS))

    def z_peer(k):
        return (yi * NZ + lax.rem(zi + k, NZ), me)

    def y_peer(k):
        return (lax.rem(yi + k, NY) * NZ + zi, me)

    cw2 = [
        pltpu.make_async_copy(
            w2_hbm.at[pl.ds(ky * 192, 192)], w2s.at[ky, pl.ds(0, 192)], wsem.at[ky]
        )
        for ky in range(3)
    ]
    cw3 = pltpu.make_async_copy(w3_hbm, w3s, wsem.at[3])
    cw4 = pltpu.make_async_copy(w4_hbm, w4s, wsem.at[4])
    cw5 = pltpu.make_async_copy(w5_hbm, w5s, wsem.at[5])
    for c in cw2 + [cw3, cw4, cw5]:
        c.start()

    barrier = pltpu.get_barrier_semaphore()
    peers = (
        [row_peer(k) for k in range(1, ROWS)]
        + [z_peer(k) for k in range(1, NZ)]
        + [y_peer(k) for k in range(1, NY)]
    )
    for peer in peers:
        pl.semaphore_signal(barrier, inc=1, device_id=peer, device_id_type=MESH)

    def beside(stage, land, n):
        up = pltpu.make_async_remote_copy(
            src_ref=stage.at[0], dst_ref=land.at[1], send_sem=ssem.at[n, 0],
            recv_sem=rsem.at[n, 1], device_id=row_peer(ROWS - 1), device_id_type=MESH,
        )
        down = pltpu.make_async_remote_copy(
            src_ref=stage.at[1], dst_ref=land.at[0], send_sem=ssem.at[n, 1],
            recv_sem=rsem.at[n, 0], device_id=row_peer(1), device_id_type=MESH,
        )
        return up, down

    def landed(land):
        top = jnp.where(me > 0, land[0].astype(F32), 0.0)
        bottom = jnp.where(me < ROWS - 1, land[1].astype(F32), 0.0)
        return top, bottom

    images = jnp.concatenate(
        [real_ref[0].reshape(48, 256), fake_ref[0].reshape(48, 256)], axis=0
    )
    for side, row in ((0, 0), (1, 15)):
        pick = onehot(iota((16, 96), 1) == iota((16, 96), 0) * 16 + row)
        stage0[side] = dot(pick, images).astype(BF)
    pl.semaphore_wait(barrier, len(peers))
    c0 = beside(stage0, land0, 0)
    for c in c0:
        c.start()

    wsm[...] = jnp.zeros_like(wsm)
    for ky in range(3):
        for kx in range(3):
            piece = w1_ref[ky, kx].astype(F32)
            for p in range(2):
                lane = (kx + p) * 128 + p * 64
                wsm[ky * 3 : ky * 3 + 3, lane : lane + 64] = piece
    small = wsm[...].astype(BF)

    def band(rr, carry):
        idx = iota((64, 16), 0)
        k = iota((64, 16), 1)
        ky = jnp.where(k >= 3, 1, 0) + jnp.where(k >= 6, 1, 0)
        ci = k - 3 * ky
        inner = (idx >> 4 == ci) & ((idx & 15) == rr + ky - 2) & (idx < 48)
        above = (idx - 48 == ci) & (rr + ky - 2 == -1)
        below = (idx - 51 == ci) & (rr + ky - 2 == 16)
        pick = onehot((inner | above | below) & (k < 9))
        block = dot(pick, small).astype(BF)
        for d in range(4):
            wb[rr, d * 64 : (d + 1) * 64, :] = block[:, d * 128 : (d + 1) * 128]
        return carry

    lax.fori_loop(0, 18, band, 0)

    for row, ref in ((0, b1_ref), (1, l1_ref)):
        vec[row : row + 1, 0:64] = ref[...]
        vec[row : row + 1, 64:128] = ref[...]
    ones_half = onehot(iota((128, 128), 0) >> 6 == iota((128, 128), 1) >> 6)
    ones_full = jnp.full((128, 128), 1.0, BF)

    def sum_half(x):
        return dot(x.astype(BF), ones_half)

    def sum_full(x):
        return dot(x.astype(BF), ones_full)

    parts[...] = jnp.zeros_like(parts)
    w2s[:, 192:256, :] = jnp.zeros((3, 64, 128), BF)

    for c in c0:
        c.wait()
    pos = iota((128, 256), 0)
    col = iota((128, 256), 1)
    base = 16 * (pos & 15) + 2 * (pos >> 4)
    take = onehot(col == base)
    edges = jnp.concatenate([land0[0], land0[1]], axis=0)
    for i, ref in ((0, real_ref), (1, fake_ref)):
        j = iota((16, 32), 0)
        k = iota((16, 32), 1)
        top = (j < 3) & (k == 3 * i + j) & (me > 0)
        bottom = (j >= 3) & (j < 6) & (k == 16 + 3 * i + j - 3) & (me < ROWS - 1)
        halo = dot(onehot(top | bottom), edges)
        whole = jnp.concatenate([ref[0].reshape(48, 256).astype(F32), halo], axis=0)
        cols = iota((64, 256), 1)
        turned = []
        for d in range(4):
            dx = d - 1
            moved = whole if dx == 0 else pltpu.roll(whole, (-dx) % 256, 1)
            moved = jnp.where((cols + dx >= 0) & (cols + dx < 256), moved, 0.0)
            turned.append(moved.astype(BF))
        tt[i] = dot_t(take, jnp.concatenate(turned, axis=0)).astype(BF)

    lane = iota((128, 128), 1)

    def put2(row, v_r, v_f):
        for i, v in ((0, v_r), (1, v_f)):
            left, right = shifted(v, 8)
            x2[i, row, :, 0:128] = jnp.where(lane < 64, left, v).astype(BF)
            x2[i, row, :, 128:256] = right.astype(BF)

    def segment1(k, message):
        bias = vec[0:1, :]
        lin = vec[1:2, :]
        sums = [0.0, 0.0]
        for i in range(2):
            weights = wb[2 * k + i + 1]
            act_r = rounded(gelu(dot(tt[0], weights) + bias))
            act_f, slope = gelu_both(dot(tt[1], weights) + bias)
            act_f = rounded(act_f)
            terms, grad = tap(act_r, act_f, lin, sum_half)
            parts[0] += fold(terms)
            a1[2 * k + i] = slope * grad
            s1[2 * k + i] = slope * 0.25
            sums[0] = sums[0] + act_r
            sums[1] = sums[1] + act_f
        v_r, v_f = [rounded((s + pltpu.roll(s, 64, 1)) * 0.25) for s in sums]
        put2(k + 1, v_r, v_f)
        if message is not None:
            stage2[message] = jnp.where(lane < 64, v_r, v_f).astype(BF)

    segment1(0, 0)
    segment1(7, 1)
    c2 = beside(stage2, land2, 1)
    for c in c2:
        c.start()

    def inner1(k, carry):
        segment1(k, None)
        return carry

    lax.fori_loop(1, 7, inner1, 0)

    for c in cw2:
        c.wait()
    for ky in range(3):
        for kx in range(3):
            piece = w2s[ky, kx * 64 : (kx + 1) * 64, :]
            w2t[ky, 0:64, kx * 128 : (kx + 1) * 128] = piece
            w2t[ky, 64:128, kx * 128 : (kx + 1) * 128] = piece
    for c in c2:
        c.wait()
    for row, v in zip((0, 9), landed(land2)):
        other = pltpu.roll(v, 64, 1)
        put2(row, jnp.where(lane < 64, v, other), jnp.where(lane < 64, other, v))

    def put(ref, i, row, v, phases, c):
        left, right = shifted(v, phases)
        ref[i, row, :, 0:c] = left.astype(BF)
        ref[i, row, :, c : 2 * c] = v.astype(BF)
        ref[i, row, :, 2 * c : 3 * c] = right.astype(BF)

    def segment2(k, message):
        acts = []
        for i in range(2):
            pre = b2_ref[...]
            for ky in range(3):
                rows = x2[i, pl.ds(2 * k + ky, 2)].reshape(256, 256)
                pre = pre + dot(rows, w2s[ky])
            if i == 0:
                acts.append(rounded(gelu(pre)))
            else:
                act, slope = gelu_both(pre)
                acts.append(rounded(act))
        terms, grad = tap(acts[0], acts[1], l2_ref[...], sum_full)
        parts[1] += fold(terms)
        a2[pl.ds(2 * k, 2)] = (slope * (4.0 * grad)).reshape(2, 128, 128)
        s2[pl.ds(2 * k, 2)] = (slope * 0.25).reshape(2, 128, 128)
        for i in range(2):
            v = rounded(pool_cols(acts[i][0:128] + acts[i][128:256], 8) * 0.25)
            put(x3, i, k + 1, v, 4, 128)
            if message is not None:
                stage3[message, :, i * 128 : (i + 1) * 128] = v.astype(BF)

    segment2(0, 0)
    segment2(3, 1)
    c3 = beside(stage3, land3, 2)
    for c in c3:
        c.start()

    def inner2(k, carry):
        segment2(k, None)
        return carry

    lax.fori_loop(1, 3, inner2, 0)

    cw3.wait()
    for c in c3:
        c.wait()
    for row, v in zip((0, 5), landed(land3)):
        for i in range(2):
            put(x3, i, row, v[:, i * 128 : (i + 1) * 128], 4, 128)
    kept3 = []
    for k in range(2):
        pre = b3_ref[...]
        for ky in range(3):
            rows = x3[:, 2 * k + ky : 2 * k + ky + 2].reshape(256, 384)
            pre = pre + dot(rows, w3s[ky * 384 : (ky + 1) * 384, :])
        act_r = rounded(gelu(pre[0:128]))
        act_f, slope = gelu_both(pre[128:256])
        act_f = rounded(act_f)
        for i, act in ((0, act_r), (1, act_f)):
            v = rounded(pool_cols(act[0:64] + act[64:128], 4) * 0.25)
            put(x4, i, k + 1, v, 2, 256)
            stage4[k, :, i * 256 : (i + 1) * 256] = v.astype(BF)
        kept3.append((act_r, act_f, slope))
    c4 = beside(stage4, land4, 3)
    for c in c4:
        c.start()
    for k, (act_r, act_f, slope) in enumerate(kept3):
        terms, grad = tap(act_r, act_f, l3_ref[...], lane_sum)
        parts[2] += fold(terms)
        a3[2 * k : 2 * k + 2] = (slope * (16.0 * grad)).reshape(2, 64, 256)
        s3[2 * k : 2 * k + 2] = (slope * 0.25).reshape(2, 64, 256)

    cw4.wait()
    for c in c4:
        c.wait()
    for row, v in zip((0, 3), landed(land4)):
        for i in range(2):
            put(x4, i, row, v[:, i * 256 : (i + 1) * 256], 2, 256)
    pre = b4_ref[...]
    for ky in range(3):
        rows = x4[:, ky : ky + 2].reshape(128, 768)
        pre = pre + dot(rows, w4s[ky * 768 : (ky + 1) * 768, :])
    act_r = rounded(gelu(pre[0:64]))
    act_f, slope = gelu_both(pre[64:128])
    act_f = rounded(act_f)
    for i, act in ((0, act_r), (1, act_f)):
        v = pool_cols(act[0:32] + act[32:64], 2) * 0.25
        stage5[:, i * 512 : (i + 1) * 512] = v.astype(BF)
    c5 = [
        pltpu.make_async_remote_copy(
            src_ref=stage5, dst_ref=land5.at[me], send_sem=gsend.at[k - 1],
            recv_sem=grecv.at[k - 1], device_id=row_peer(k), device_id_type=MESH,
        )
        for k in range(1, ROWS)
    ]
    for c in c5:
        c.start()
    land5[me] = stage5[...]
    terms, grad = tap(act_r, act_f, l4_ref[...], lane_sum)
    parts[3] += fold(terms)
    a4[...] = (slope * (64.0 * grad)).reshape(2, 32, 512)
    s4[...] = (slope * 0.25).reshape(2, 32, 512)

    zero_row = jnp.zeros((16, 1536), BF)
    for row in (0, 9):
        x5[0, row] = zero_row
        x5[1, row] = zero_row
        g5[row] = zero_row
    cw5.wait()
    for c in c5:
        c.wait()

    def fill5(row, carry):
        v = land5[row].astype(F32)
        for i in range(2):
            put(x5, i, row + 1, v[:, i * 512 : (i + 1) * 512], 1, 512)
        return carry

    lax.fori_loop(0, ROWS, fill5, 0)
    pre = b5_ref[...]
    for ky in range(3):
        rows = x5[:, ky : ky + 8].reshape(256, 1536)
        pre = pre + dot(rows, w5s[ky * 1536 : (ky + 1) * 1536, :])
    act_r = rounded(gelu(pre[0:128]))
    act_f, slope = gelu_both(pre[128:256])
    act_f = rounded(act_f)
    terms, grad = tap(act_r, act_f, l5_ref[...], lane_sum)
    parts[4] += fold(terms) * 0.125
    gpre = rounded(slope * (256.0 * grad))

    def put_back(ref, row, v, phases, c):
        left, right = shifted(v, phases)
        ref[row, :, 0:c] = right.astype(BF)
        ref[row, :, c : 2 * c] = v.astype(BF)
        ref[row, :, 2 * c : 3 * c] = left.astype(BF)

    for row in range(ROWS):
        put_back(g5, row + 1, gpre[row * 16 : (row + 1) * 16], 1, 512)

    def spread_loss(src, land, slot, peer, count, first):
        copies = [
            pltpu.make_async_remote_copy(
                src_ref=src, dst_ref=land.at[slot], send_sem=lsend.at[first + k],
                recv_sem=lrecv.at[first + k], device_id=peer(k), device_id_type=MESH,
            )
            for k in range(1, count)
        ]
        for c in copies:
            c.start()
        land[slot] = src[...]
        return copies

    def gathered_loss(copies, land, count):
        for c in copies:
            c.wait()
        total = land[0]
        for j in range(1, count):
            total = total + land[j]
        return total

    rows_of = iota((8, 128), 0)
    mine = jnp.zeros((8, 128), F32)
    for s in range(5):
        mine = mine + jnp.where(rows_of == s, jnp.sum(parts[s], axis=0, keepdims=True), 0.0)
    own[0] = mine
    cl = spread_loss(own.at[0], lrow, me, row_peer, ROWS, 0)

    gin = jnp.zeros((16, 512), F32)
    for ky in range(3):
        rows = g5[me + 2 - ky]
        for kx in range(3):
            n = (ky * 3 + kx) * 512
            gin = gin + dot_t(rows[:, kx * 512 : (kx + 1) * 512], w5s[n : n + 512, :])

    wide = spread_cols(gin, 1)
    for j in range(2):
        v = rounded(a4[j] + s4[j] * wide)
        bs4[j] = v.astype(BF)
        put_back(g4, j + 1, v, 2, 512)
    cb4 = beside(bs4, bl4, 4)
    for c in cb4:
        c.start()
    own[1] = gathered_loss(cl, lrow, ROWS)
    cl = spread_loss(own.at[1], lz, zi, z_peer, NZ, 8)
    for c in cb4:
        c.wait()
    for row, v in zip((0, 3), landed(bl4)):
        put_back(g4, row, v, 2, 512)
    gin = jnp.zeros((64, 256), F32)
    for ky in range(3):
        rows = g4[2 - ky : 4 - ky].reshape(64, 1536)
        for kx in range(3):
            n = (ky * 3 + kx) * 256
            gin = gin + dot_t(rows[:, kx * 512 : (kx + 1) * 512], w4s[n : n + 256, :])

    for k in range(2):
        wide = spread_cols(gin[k * 32 : (k + 1) * 32], 2)
        for j in (2 * k, 2 * k + 1):
            v = rounded(a3[j] + s3[j] * wide)
            put_back(g3, j + 1, v, 4, 256)
            if j == 0:
                bs3[0] = v.astype(BF)
            if j == 3:
                bs3[1] = v.astype(BF)
    cb3 = beside(bs3, bl3, 5)
    for c in cb3:
        c.start()

    def back3(slab):
        out = 0.0
        for ky in range(3):
            rows = slab(ky)
            for kx in range(3):
                n = (ky * 3 + kx) * 128
                out = out + dot_t(rows[:, kx * 256 : (kx + 1) * 256], w3s[n : n + 128, :])
        return out

    def to2(row, g, side):
        wide = spread_cols(g, 4)
        for j in range(2):
            v = rounded(a2[2 * row + j] + s2[2 * row + j] * wide)
            put_back(g2, 2 * row + j + 1, v, 8, 128)
            if side == j:
                bs2[side] = v.astype(BF)

    gin = back3(lambda ky: g3[3 - ky : 5 - ky].reshape(128, 768))
    to2(1, gin[0:64], None)
    to2(2, gin[64:128], None)
    own[2] = gathered_loss(cl, lz, NZ)
    cl = spread_loss(own.at[2], ly, yi, y_peer, NY, 16)
    for c in cb3:
        c.wait()
    for row, v in zip((0, 5), landed(bl3)):
        put_back(g3, row, v, 4, 256)
    gin = back3(lambda ky: jnp.concatenate([g3[2 - ky], g3[5 - ky]], axis=0))
    to2(0, gin[0:64], 0)
    to2(3, gin[64:128], 1)
    cb2 = beside(bs2, bl2, 6)
    for c in cb2:
        c.start()

    def back2(row, side):
        g = 0.0
        for ky in range(3):
            g = g + dot_t(g2[row + 2 - ky], w2t[ky])
        for j in range(2):
            v = (a1[2 * row + j] + s1[2 * row + j] * g).astype(BF)
            gp1[2 * row + j + 1] = v
            if side == j:
                bs1[side] = v

    def inner_back2(row, carry):
        back2(row, None)
        return carry

    lax.fori_loop(1, 7, inner_back2, 0)
    for c in cb2:
        c.wait()
    for row, v in zip((0, 9), landed(bl2)):
        put_back(g2, row, v, 8, 128)
    back2(0, 0)
    back2(7, 1)
    cb1 = beside(bs1, bl1, 7)
    for c in cb1:
        c.start()

    g = jnp.zeros((128, 256), F32)
    for rr in range(1, 17):
        g = g + dot_t(gp1[rr], wb[rr])
    total = gathered_loss(cl, ly, NY)
    sums = jnp.sum(total, axis=1, keepdims=True)
    lanes = iota((8, 128), 1)
    counts = [32.0 * (128 >> s) * (256 >> s) for s in range(5)]
    scale = jnp.zeros((8, 128), F32)
    for s in range(5):
        scale = scale + jnp.where((lanes == s) & (rows_of == s), 1.0 / counts[s], 0.0)
    loss_ref[...] = jnp.sum(sums * scale, axis=0, keepdims=True)[:, 0:5]
    for c in cb1:
        c.wait()
    for rr, v in zip((0, 17), landed(bl1)):
        g = g + dot_t(v.astype(BF), wb[rr])
    across = jnp.transpose(g)
    lined = jnp.concatenate([across[d * 64 : (d + 1) * 64] for d in range(4)], axis=1)
    back = jnp.concatenate([onehot(col == base + d - 1) for d in range(4)], axis=0)
    high = lined.astype(BF)
    low = (lined - high.astype(F32)).astype(BF)
    out = dot(high, back) + dot(low, back)
    grad_ref[0] = out[0:48].reshape(3, 16, 256)


def on_device(*args):
    (real, fake, w1, w2, w3, w4, w5, *vectors) = args
    flat = [w.reshape(-1, w.shape[-1]) for w in (w2, w3, w4, w5)]
    vectors = [v.reshape(1, -1) for v in vectors]
    vmem = pl.BlockSpec(memory_space=pltpu.VMEM)
    anywhere = pl.BlockSpec(memory_space=pl.ANY)
    v = pltpu.VMEM
    dma = pltpu.SemaphoreType.DMA
    scratch = [
        v((3, 256, 128), BF), v((3, 128, 384), BF), v((1152, 256), BF), v((2304, 512), BF),
        v((4608, 512), BF), v((16, 512), F32), v((18, 256, 128), BF), v((8, 128), F32),
        v((2, 128, 256), BF),
        v((2, 10, 128, 256), BF), v((2, 6, 64, 384), BF), v((2, 4, 32, 768), BF),
        v((2, 10, 16, 1536), BF),
        v((10, 128, 384), BF), v((6, 64, 768), BF), v((4, 32, 1536), BF), v((10, 16, 1536), BF),
        v((18, 128, 128), BF),
        v((16, 128, 128), F32), v((16, 128, 128), F32), v((8, 128, 128), F32),
        v((8, 128, 128), F32), v((4, 64, 256), F32), v((4, 64, 256), F32),
        v((2, 32, 512), F32), v((2, 32, 512), F32),
        v((2, 16, 256), BF), v((2, 16, 256), BF), v((2, 128, 128), BF), v((2, 128, 128), BF),
        v((2, 64, 256), BF), v((2, 64, 256), BF), v((2, 32, 512), BF), v((2, 32, 512), BF),
        v((8, 16, 1024), BF), v((16, 1024), BF),
        v((2, 32, 512), BF), v((2, 32, 512), BF), v((2, 64, 256), BF), v((2, 64, 256), BF),
        v((2, 128, 128), BF), v((2, 128, 128), BF), v((2, 128, 128), BF), v((2, 128, 128), BF),
        v((5, 8, 128), F32), v((3, 8, 128), F32), v((8, 8, 128), F32), v((8, 8, 128), F32),
        v((4, 8, 128), F32),
        dma((6,)), dma((8, 2)), dma((8, 2)), dma((7,)), dma((7,)), dma((24,)), dma((24,)),
    ]
    losses, grads = pl.pallas_call(
        body,
        out_shape=(
            jax.ShapeDtypeStruct((1, 5), F32),
            jax.ShapeDtypeStruct((1, 3, 16, 256), F32),
        ),
        in_specs=[vmem] * 3 + [anywhere] * 4 + [vmem] * 10,
        out_specs=(vmem, vmem),
        scratch_shapes=scratch,
        compiler_params=pltpu.CompilerParams(
            collective_id=0, has_side_effects=True, vmem_limit_bytes=56 << 20
        ),
        name="whole_step",
    )(real, fake, w1, *flat, *vectors)
    return (losses.reshape(5), grads)


def solution(mesh):
    frames = P("dp", None, "rows", None)
    return jax.shard_map(
        on_device,
        mesh=mesh,
        in_specs=(frames, frames) + (P(),) * 15,
        out_specs=(P(), frames),
        check_vma=False,
    )
```

```python
import functools

import jax
import jax.numpy as jnp
from jax import lax
from jax.experimental import pallas as pl
from jax.experimental.pallas import tpu as pltpu
from jax.sharding import PartitionSpec as P

MESH = pl.DeviceIdType.MESH
F32 = jnp.float32
BF = jnp.bfloat16
EPS = 1e-06
ROOT = 0.7978845608028654
CUBE = 0.044715

ROWS = 8
NZ = 8
NY = 4


def dot(a, b):
    return lax.dot_general(a, b, (((1,), (0,)), ((), ())), preferred_element_type=F32)


def dot_t(a, b):
    return lax.dot_general(a, b, (((1,), (1,)), ((), ())), preferred_element_type=F32)


def iota(shape, dim):
    return lax.broadcasted_iota(jnp.int32, shape, dim)


def onehot(cond):
    return jnp.where(cond, 1.0, 0.0).astype(BF)


def rounded(x):
    return x.astype(BF).astype(F32)


def gelu(x):
    t = jnp.tanh(x * (ROOT + (ROOT * CUBE) * (x * x)))
    return x * (0.5 + 0.5 * t)


def gelu_both(x):
    x2 = x * x
    t = jnp.tanh(x * (ROOT + (ROOT * CUBE) * x2))
    h = 0.5 + 0.5 * t
    slope = h + (0.5 * x) * (1.0 - t * t) * (ROOT + (3.0 * ROOT * CUBE) * x2)
    return x * h, slope


def tap(r, f, lin, total):
    a = lax.rsqrt(total(r * r) + EPS)
    b = lax.rsqrt(total(f * f) + EPS)
    nf = f * b
    d = r * a - nf
    ld = lin * d
    grad = (ld - nf * total(nf * ld)) * (-2.0 * b)
    return ld * d, grad


def lane_sum(x):
    return jnp.sum(x, axis=-1, keepdims=True)


def fold(x):
    m, c = x.shape
    y = jnp.sum(x.reshape(m // 8, 8, c), axis=0)
    out = y[:, 0:128]
    for j in range(1, c // 128):
        out = out + y[:, j * 128 : (j + 1) * 128]
    return out


def shifted(v, phases):
    c = v.shape[-1]
    q = iota((16, c), 0)
    n = phases * 16
    tail = jnp.where(q < 15, pltpu.roll(v[0:16], 15, 0), 0.0)
    head = jnp.where(q > 0, pltpu.roll(v[n - 16 : n], 1, 0), 0.0)
    if phases == 1:
        return head, tail
    left = jnp.concatenate([head, v[0 : n - 16]], axis=0)
    right = jnp.concatenate([v[16:n], tail], axis=0)
    return left, right


def pool_cols(v, phases):
    c = v.shape[-1]
    return jnp.sum(v.reshape(phases // 2, 2, 16, c), axis=1).reshape(phases * 8, c)


def spread_cols(v, phases):
    c = v.shape[-1]
    y = jnp.broadcast_to(v.reshape(phases, 1, 16, c), (phases, 2, 16, c))
    return y.reshape(phases * 32, c)


def body(
    real_ref, fake_ref, w1_ref, w2_hbm, w3_hbm, w4_hbm, w5_hbm,
    b1_ref, b2_ref, b3_ref, b4_ref, b5_ref, l1_ref, l2_ref, l3_ref, l4_ref, l5_ref,
    loss_ref, grad_ref,
    w2s, w2t, w3s, w4s, w5s, wsm, wb, vec, tt,
    x2, x3, x4, x5, g2, g3, g4, g5, gp1,
    act1, sl1, act2, sl2, act3, sl3,
    a1, s1, a2, s2, a3, s3, a4, s4,
    stage0, land0, stage5, land5, stage4, land4,
    parts, own, lrow, lz, ly,
    wsem, ssem, rsem, gsend, grecv, lsend, lrecv,
):
    dp = lax.axis_index("dp")
    me = lax.axis_index("rows")
    zi = lax.rem(dp, NZ)
    yi = lax.div(dp, NZ)
    not_first = me > 0
    not_last = me < ROWS - 1

    def row_peer(k):
        return (dp, lax.rem(me + k, ROWS))

    def z_peer(k):
        return (yi * NZ + lax.rem(zi + k, NZ), me)

    def y_peer(k):
        return (lax.rem(yi + k, NY) * NZ + zi, me)

    cw2 = [
        pltpu.make_async_copy(
            w2_hbm.at[pl.ds(ky * 192, 192)], w2s.at[ky, pl.ds(0, 192)], wsem.at[ky]
        )
        for ky in range(3)
    ]
    cw3 = pltpu.make_async_copy(w3_hbm, w3s, wsem.at[3])
    cw4 = pltpu.make_async_copy(w4_hbm, w4s, wsem.at[4])
    cw5 = pltpu.make_async_copy(w5_hbm, w5s, wsem.at[5])
    for c in cw2 + [cw3, cw4, cw5]:
        c.start()

    barrier = pltpu.get_barrier_semaphore()
    peers = (
        [row_peer(k) for k in range(1, ROWS)]
        + [z_peer(k) for k in range(1, NZ)]
        + [y_peer(k) for k in range(1, NY)]
    )
    for peer in peers:
        pl.semaphore_signal(barrier, inc=1, device_id=peer, device_id_type=MESH)

    def beside(first, second, land, n):
        up = pltpu.make_async_remote_copy(
            src_ref=first, dst_ref=land.at[1], send_sem=ssem.at[n, 0],
            recv_sem=rsem.at[n, 1], device_id=row_peer(ROWS - 1), device_id_type=MESH,
        )
        down = pltpu.make_async_remote_copy(
            src_ref=second, dst_ref=land.at[0], send_sem=ssem.at[n, 1],
            recv_sem=rsem.at[n, 0], device_id=row_peer(1), device_id_type=MESH,
        )
        return up, down

    stage0[0:48] = real_ref[0].reshape(48, 256)
    stage0[48:96] = fake_ref[0].reshape(48, 256)

    wsm[...] = jnp.zeros_like(wsm)
    for ky in range(3):
        for kx in range(3):
            piece = w1_ref[ky, kx].astype(F32)
            for p in range(2):
                lane = (kx + p) * 128 + p * 64
                wsm[ky * 3 : ky * 3 + 3, lane : lane + 64] = piece
    small = wsm[...].astype(BF)

    def band(k, carry):
        idx = iota((64, 16), 0)
        n = iota((64, 16), 1)
        ky = jnp.where(n >= 3, 1, 0) + jnp.where(n >= 6, 1, 0)
        ci = n - 3 * ky
        for half in range(2):
            row = jnp.where(k < 8, 2 * k + half, 17 * half - 1)
            at = row + ky - 1
            inner = (idx >> 4 == ci) & ((idx & 15) == at) & (idx < 48)
            above = (idx - 48 == ci) & (at == -1)
            below = (idx - 51 == ci) & (at == 16)
            block = dot(onehot((inner | above | below) & (n < 9)), small).astype(BF)
            for d in range(4):
                wb[k, d * 64 : (d + 1) * 64, half * 128 : (half + 1) * 128] = block[
                    :, d * 128 : (d + 1) * 128
                ]
        return carry

    lax.fori_loop(0, 9, band, 0)

    for row, ref in ((0, b1_ref), (1, l1_ref)):
        for q in range(4):
            vec[row : row + 1, q * 64 : (q + 1) * 64] = ref[...]
    ones_part = onehot(iota((256, 256), 0) >> 6 == iota((256, 256), 1) >> 6)
    ones_full = jnp.full((128, 128), 1.0, BF)

    def sum_part(x):
        return dot(x.astype(BF), ones_part)

    def sum_full(x):
        return dot(x.astype(BF), ones_full)

    parts[...] = jnp.zeros_like(parts)
    w2s[:, 192:256, :] = jnp.zeros((3, 64, 128), BF)

    pos = iota((128, 256), 0)
    col = iota((128, 256), 1)
    base = 16 * (pos & 15) + 2 * (pos >> 4)
    take = onehot(col == base)

    def patches(slot, images, sources):
        for i in range(2):
            halo = jnp.zeros((16, 256), F32)
            for source, row, off, ok in sources:
                j = iota((16, 96), 0) - off
                k = iota((16, 96), 1)
                pick = (j >= 0) & (j < 3) & (k == i * 48 + j * 16 + row)
                if ok is not None:
                    pick = pick & ok
                halo = halo + dot(onehot(pick), source)
            whole = jnp.concatenate([images[i * 48 : (i + 1) * 48].astype(F32), halo], axis=0)
            cols = iota((64, 256), 1)
            turned = []
            for d in range(4):
                dx = d - 1
                moved = whole if dx == 0 else pltpu.roll(whole, (-dx) % 256, 1)
                moved = jnp.where((cols + dx >= 0) & (cols + dx < 256), moved, 0.0)
                turned.append(moved.astype(BF))
            tt[slot, i * 128 : (i + 1) * 128, :] = dot_t(
                take, jnp.concatenate(turned, axis=0)
            ).astype(BF)

    mine = stage0[...]
    patches(0, mine, ())

    pl.semaphore_wait(barrier, len(peers))
    c0 = beside(stage0, stage0, land0, 0)
    for c in c0:
        c.start()

    lane = iota((128, 128), 1)
    bias1 = vec[0:1, :]
    lin1 = vec[1:2, :]

    def put2(row, v):
        for i in range(2):
            w = v[i * 128 : (i + 1) * 128]
            left, right = shifted(w, 8)
            x2[row, i * 128 : (i + 1) * 128, 0:128] = jnp.where(lane < 64, left, w).astype(BF)
            x2[row, i * 128 : (i + 1) * 128, 128:256] = right.astype(BF)

    def segment1(slot, k, p, keep, ok):
        pre = dot(tt[slot], wb[k]) + bias1
        if keep is None:
            act = rounded(gelu(pre))
        else:
            act_f, slope = gelu_both(pre[128:256])
            act = rounded(jnp.concatenate([gelu(pre[0:128]), act_f], axis=0))
            if keep == "left":
                act1[8, :, 0:128] = act[:, 128:256].astype(BF)
                sl1[8, :, 0:128] = slope[:, 128:256]
            elif keep == "right":
                act1[8, :, 128:256] = act[:, 0:128].astype(BF)
                sl1[8, :, 128:256] = slope[:, 0:128]
            else:
                act1[k] = act.astype(BF)
                sl1[k] = slope
        s = act[:, 0:128] + act[:, 128:256]
        v = rounded((s + pltpu.roll(s, 64, 1)) * 0.25)
        if ok is not None:
            v = jnp.where(ok, v, 0.0)
        put2(p, v)

    def tap1(k, counted):
        act = act1[k].astype(F32)
        terms, grad = tap(act[0:128], act[128:256], lin1, sum_part)
        if counted:
            parts[0] += fold(terms)
        slope = sl1[k]
        a1[k] = slope * grad
        s1[k] = slope * 0.25

    def inner1(n, carry):
        for j in range(2):
            k = 1 + 2 * n + j
            segment1(0, k, 7 + k, "own", None)
        return carry

    lax.fori_loop(0, 3, inner1, 0)

    def inner_tap1(n, carry):
        for j in range(2):
            tap1(1 + 2 * n + j, True)
        return carry

    lax.fori_loop(0, 3, inner_tap1, 0)

    for c in cw2:
        c.wait()
    for ky in range(3):
        for kx in range(3):
            piece = w2s[ky, kx * 64 : (kx + 1) * 64, :]
            w2t[ky, 0:64, kx * 128 : (kx + 1) * 128] = piece
            w2t[ky, 64:128, kx * 128 : (kx + 1) * 128] = piece

    for c in c0:
        c.wait()
    upper = land0[0]
    lower = land0[1]
    patches(1, mine, ((upper, 15, 0, not_first), (lower, 0, 3, not_last)))
    patches(2, upper, ((mine, 0, 3, None),))
    patches(3, lower, ((mine, 15, 0, None),))
    segment1(2, 7, 6, "left", not_first)
    segment1(1, 0, 7, "own", None)
    segment1(1, 7, 14, "own", None)
    segment1(3, 0, 15, "right", not_last)

    def outer1(n, carry):
        for j in range(2):
            k = 1 + 2 * n + j
            segment1(2, k, k - 1, None, not_first)
            segment1(3, k, 15 + k, None, not_last)
        return carry

    lax.fori_loop(0, 3, outer1, 0)

    def put(ref, row, v, phases, c):
        n = phases * 16
        for i in range(2):
            w = v[i * n : (i + 1) * n]
            left, right = shifted(w, phases)
            ref[row, i * n : (i + 1) * n, 0:c] = left.astype(BF)
            ref[row, i * n : (i + 1) * n, c : 2 * c] = w.astype(BF)
            ref[row, i * n : (i + 1) * n, 2 * c : 3 * c] = right.astype(BF)

    def both(pre, n):
        parts_of = []
        slopes = []
        for row in range(2):
            top = 2 * row * n
            parts_of.append(gelu(pre[top : top + n]))
            act, slope = gelu_both(pre[top + n : top + 2 * n])
            parts_of.append(act)
            slopes.append(slope)
        return rounded(jnp.concatenate(parts_of, axis=0)), jnp.concatenate(slopes, axis=0)

    def segment2(m):
        pre = b2_ref[...]
        for ky in range(3):
            rows = x2[pl.ds(2 * m + ky, 2)].reshape(512, 256)
            pre = pre + dot(rows, w2s[ky])
        act, slope = both(pre, 128)
        act2[m] = act.astype(BF)
        sl2[m] = slope
        v = rounded(pool_cols(act[0:256] + act[256:512], 16) * 0.25)
        ok = ((m >= 3) | not_first) & ((m < 7) | not_last)
        put(x3, m, jnp.where(ok, v, 0.0), 4, 128)

    def loop2(n, carry):
        for j in range(2):
            segment2(2 * n + j)
        return carry

    lax.fori_loop(0, 5, loop2, 0)

    cw3.wait()

    def segment3(n):
        pre = b3_ref[...]
        for ky in range(3):
            rows = x3[pl.ds(2 * n + ky, 2)].reshape(256, 384)
            pre = pre + dot(rows, w3s[ky * 384 : (ky + 1) * 384, :])
        act, slope = both(pre, 64)
        act3[n] = act.astype(BF)
        sl3[n] = slope
        v = rounded(pool_cols(act[0:128] + act[128:256], 8) * 0.25)
        ok = ((n >= 1) | not_first) & ((n < 3) | not_last)
        put(x4, n, jnp.where(ok, v, 0.0), 2, 256)

    def loop3(n, carry):
        for j in range(2):
            segment3(2 * n + j)
        return carry

    lax.fori_loop(0, 2, loop3, 0)

    cw4.wait()
    pre = b4_ref[...]
    for ky in range(3):
        rows = x4[ky : ky + 2].reshape(128, 768)
        pre = pre + dot(rows, w4s[ky * 768 : (ky + 1) * 768, :])
    act, slope = both(pre, 32)
    stage5[...] = (pool_cols(act[0:64] + act[64:128], 4) * 0.25).astype(BF)
    c5 = [
        pltpu.make_async_remote_copy(
            src_ref=stage5, dst_ref=land5.at[me], send_sem=gsend.at[k - 1],
            recv_sem=grecv.at[k - 1], device_id=row_peer(k), device_id_type=MESH,
        )
        for k in range(1, ROWS)
    ]
    for c in c5:
        c.start()
    land5[me] = stage5[...]

    act = act.reshape(2, 2, 32, 512)
    terms, grad = tap(
        act[:, 0].reshape(64, 512), act[:, 1].reshape(64, 512), l4_ref[...], lane_sum
    )
    parts[3] += fold(terms)
    a = slope * (64.0 * grad)
    s = slope * 0.25
    a4[...] = a.reshape(2, 32, 512)
    s4[...] = s.reshape(2, 32, 512)
    stage4[0:2] = a.astype(BF).reshape(2, 32, 512)
    stage4[2:4] = s.astype(BF).reshape(2, 32, 512)
    c4 = beside(stage4, stage4, land4, 1)
    for c in c4:
        c.start()

    def tap3(n, counted):
        act = act3[n].astype(F32).reshape(2, 2, 64, 256)
        slope = sl3[n]
        terms, grad = tap(
            act[:, 0].reshape(128, 256), act[:, 1].reshape(128, 256), l3_ref[...], lane_sum
        )
        if counted:
            parts[2] += fold(terms)
        a3[2 * n : 2 * n + 2] = (slope * (16.0 * grad)).reshape(2, 64, 256)
        s3[2 * n : 2 * n + 2] = (slope * 0.25).reshape(2, 64, 256)

    def tap2(m, counted):
        act = act2[m].astype(F32).reshape(2, 2, 128, 128)
        slope = sl2[m]
        terms, grad = tap(
            act[:, 0].reshape(256, 128), act[:, 1].reshape(256, 128), l2_ref[...], sum_full
        )
        if counted:
            parts[1] += fold(terms)
        a2[pl.ds(2 * m - 4, 2)] = (slope * (4.0 * grad)).reshape(2, 128, 128)
        s2[pl.ds(2 * m - 4, 2)] = (slope * 0.25).reshape(2, 128, 128)

    tap1(0, True)
    tap1(7, True)
    tap1(8, False)
    tap3(1, True)
    tap3(2, True)

    def loop_tap2(n, carry):
        for j in range(2):
            tap2(3 + 2 * n + j, True)
        return carry

    lax.fori_loop(0, 2, loop_tap2, 0)

    def spread_loss(src, land, slot, peer, count, first):
        copies = [
            pltpu.make_async_remote_copy(
                src_ref=src, dst_ref=land.at[slot], send_sem=lsend.at[first + k],
                recv_sem=lrecv.at[first + k], device_id=peer(k), device_id_type=MESH,
            )
            for k in range(1, count)
        ]
        for c in copies:
            c.start()
        land[slot] = src[...]
        return copies

    def gathered_loss(copies, land, count):
        for c in copies:
            c.wait()
        total = land[0]
        for j in range(1, count):
            total = total + land[j]
        return total

    rows_of = iota((8, 128), 0)
    sums = jnp.zeros((8, 128), F32)
    for s in range(4):
        sums = sums + jnp.where(rows_of == s, jnp.sum(parts[s], axis=0, keepdims=True), 0.0)
    own[0] = sums
    cl = spread_loss(own.at[0], lrow, me, row_peer, ROWS, 0)

    tap2(2, False)
    tap2(7, False)
    tap3(0, False)
    tap3(3, False)

    for row in (0, 9):
        x5[row] = jnp.zeros((32, 1536), BF)
    for row in (0, 1, 10, 11):
        g5[row] = jnp.zeros((16, 1536), BF)
    cw5.wait()
    for c in c5:
        c.wait()
    for row in range(ROWS):
        put(x5, row + 1, land5[row].astype(F32), 1, 512)
    pre = b5_ref[...]
    for ky in range(3):
        rows = x5[ky : ky + 8].reshape(256, 1536)
        pre = pre + dot(rows, w5s[ky * 1536 : (ky + 1) * 1536, :])
    pre = pre.reshape(8, 2, 16, 512)
    act_r = rounded(gelu(pre[:, 0].reshape(128, 512)))
    act_f, slope = gelu_both(pre[:, 1].reshape(128, 512))
    act_f = rounded(act_f)
    terms, grad = tap(act_r, act_f, l5_ref[...], lane_sum)
    gpre = rounded(slope * (256.0 * grad))

    def put_back(ref, row, v, phases, c):
        left, right = shifted(v, phases)
        ref[row, :, 0:c] = right.astype(BF)
        ref[row, :, c : 2 * c] = v.astype(BF)
        ref[row, :, 2 * c : 3 * c] = left.astype(BF)

    for row in range(ROWS):
        put_back(g5, row + 2, gpre[row * 16 : (row + 1) * 16], 1, 512)
    fifth = jnp.sum(fold(terms), axis=0, keepdims=True)
    own[1] = gathered_loss(cl, lrow, ROWS) + jnp.where(rows_of == 4, fifth, 0.0)
    cl = spread_loss(own.at[1], lz, zi, z_peer, NZ, 8)

    gin = jnp.zeros((48, 512), F32)
    for ky in range(3):
        rows = g5[pl.ds(me + 2 - ky, 3)].reshape(48, 1536)
        for kx in range(3):
            n = (ky * 3 + kx) * 512
            gin = gin + dot_t(rows[:, kx * 512 : (kx + 1) * 512], w5s[n : n + 512, :])

    for c in c4:
        c.wait()
    for u in range(6):
        wide = spread_cols(gin[(u // 2) * 16 : (u // 2 + 1) * 16], 1)
        if 2 <= u < 4:
            v = a4[u - 2] + s4[u - 2] * wide
        else:
            side, j, ok = (0, u, not_first) if u < 2 else (1, u - 4, not_last)
            a = land4[side, j].astype(F32)
            s = land4[side, 2 + j].astype(F32)
            v = jnp.where(ok, a + s * wide, 0.0)
        put_back(g4, u, rounded(v), 2, 512)
    gin = jnp.zeros((128, 256), F32)
    for ky in range(3):
        rows = g4[2 - ky : 6 - ky].reshape(128, 1536)
        for kx in range(3):
            n = (ky * 3 + kx) * 256
            gin = gin + dot_t(rows[:, kx * 512 : (kx + 1) * 512], w4s[n : n + 256, :])

    for j in range(8):
        wide = spread_cols(gin[(j // 2) * 32 : (j // 2 + 1) * 32], 2)
        v = a3[j] + s3[j] * wide
        if j < 2:
            v = jnp.where(not_first, v, 0.0)
        if j >= 6:
            v = jnp.where(not_last, v, 0.0)
        put_back(g3, j, rounded(v), 4, 256)
    gin = 0.0
    for ky in range(3):
        rows = g3[2 - ky : 8 - ky].reshape(384, 768)
        for kx in range(3):
            n = (ky * 3 + kx) * 128
            gin = gin + dot_t(rows[:, kx * 256 : (kx + 1) * 256], w3s[n : n + 128, :])
    own[2] = gathered_loss(cl, lz, NZ)
    cl = spread_loss(own.at[2], ly, yi, y_peer, NY, 16)

    for j in range(12):
        wide = spread_cols(gin[(j // 2) * 64 : (j // 2 + 1) * 64], 4)
        v = a2[j] + s2[j] * wide
        if j < 2:
            v = jnp.where(not_first, v, 0.0)
        if j >= 10:
            v = jnp.where(not_last, v, 0.0)
        put_back(g2, j, rounded(v), 8, 128)

    def inner_back2(n, carry):
        g = 0.0
        for ky in range(3):
            rows = g2[pl.ds(2 * n + 3 - ky, 2)].reshape(256, 384)
            g = g + dot_t(rows, w2t[ky])
        for j in range(2):
            k = 2 * n + j
            one = g[j * 128 : (j + 1) * 128]
            wide = jnp.concatenate([one, one], axis=1)
            gp1[k] = (a1[k] + s1[k] * wide).astype(BF)
        return carry

    lax.fori_loop(0, 4, inner_back2, 0)
    g = 0.0
    for ky in range(3):
        rows = jnp.concatenate([g2[2 - ky], g2[11 - ky]], axis=0)
        g = g + dot_t(rows, w2t[ky])
    above = jnp.where(not_first, a1[8, :, 0:128] + s1[8, :, 0:128] * g[0:128], 0.0)
    below = jnp.where(not_last, a1[8, :, 128:256] + s1[8, :, 128:256] * g[128:256], 0.0)
    gp1[8] = jnp.concatenate([above, below], axis=1).astype(BF)

    g = jnp.zeros((128, 256), F32)
    for k in range(9):
        g = g + dot_t(gp1[k], wb[k])
    across = jnp.transpose(g)
    lined = jnp.concatenate([across[d * 64 : (d + 1) * 64] for d in range(4)], axis=1)
    back = jnp.concatenate([onehot(col == base + d - 1) for d in range(4)], axis=0)
    high = lined.astype(BF)
    low = (lined - high.astype(F32)).astype(BF)
    out = dot(high, back) + dot(low, back)
    grad_ref[0] = out[0:48].reshape(3, 16, 256)

    total = gathered_loss(cl, ly, NY)
    sums = jnp.sum(total, axis=1, keepdims=True)
    lanes = iota((8, 128), 1)
    counts = [32.0 * (128 >> s) * (256 >> s) for s in range(5)]
    scale = jnp.zeros((8, 128), F32)
    for s in range(5):
        scale = scale + jnp.where((lanes == s) & (rows_of == s), 1.0 / counts[s], 0.0)
    loss_ref[...] = jnp.sum(sums * scale, axis=0, keepdims=True)[:, 0:5]


def on_device(*args):
    (real, fake, w1, w2, w3, w4, w5, *vectors) = args
    flat = [w.reshape(-1, w.shape[-1]) for w in (w2, w3, w4, w5)]
    vectors = [v.reshape(1, -1) for v in vectors]
    vmem = pl.BlockSpec(memory_space=pltpu.VMEM)
    anywhere = pl.BlockSpec(memory_space=pl.ANY)
    v = pltpu.VMEM
    dma = pltpu.SemaphoreType.DMA
    scratch = [
        v((3, 256, 128), BF), v((3, 128, 384), BF), v((1152, 256), BF), v((2304, 512), BF),
        v((4608, 512), BF), v((16, 512), F32), v((9, 256, 256), BF), v((8, 256), F32),
        v((4, 256, 256), BF),
        v((22, 256, 256), BF), v((10, 128, 384), BF), v((4, 64, 768), BF), v((10, 32, 1536), BF),
        v((12, 128, 384), BF), v((8, 64, 768), BF), v((6, 32, 1536), BF), v((12, 16, 1536), BF),
        v((9, 128, 256), BF),
        v((9, 256, 256), BF), v((9, 128, 256), F32), v((10, 512, 128), BF),
        v((10, 256, 128), F32), v((4, 256, 256), BF), v((4, 128, 256), F32),
        v((9, 128, 256), F32), v((9, 128, 256), F32), v((12, 128, 128), F32),
        v((12, 128, 128), F32), v((8, 64, 256), F32), v((8, 64, 256), F32),
        v((2, 32, 512), F32), v((2, 32, 512), F32),
        v((96, 256), BF), v((2, 96, 256), BF), v((32, 512), BF), v((8, 32, 512), BF),
        v((4, 32, 512), BF), v((2, 4, 32, 512), BF),
        v((5, 8, 128), F32), v((3, 8, 128), F32), v((8, 8, 128), F32), v((8, 8, 128), F32),
        v((4, 8, 128), F32),
        dma((6,)), dma((2, 2)), dma((2, 2)), dma((7,)), dma((7,)), dma((24,)), dma((24,)),
    ]
    losses, grads = pl.pallas_call(
        body,
        out_shape=(
            jax.ShapeDtypeStruct((1, 5), F32),
            jax.ShapeDtypeStruct((1, 3, 16, 256), F32),
        ),
        in_specs=[vmem] * 3 + [anywhere] * 4 + [vmem] * 10,
        out_specs=(vmem, vmem),
        scratch_shapes=scratch,
        compiler_params=pltpu.CompilerParams(
            collective_id=0, has_side_effects=True, vmem_limit_bytes=56 << 20
        ),
        name="whole_step",
    )(real, fake, w1, *flat, *vectors)
    return (losses.reshape(5), grads)


def solution(mesh):
    frames = P("dp", None, "rows", None)
    return jax.shard_map(
        on_device,
        mesh=mesh,
        in_specs=(frames, frames) + (P(),) * 15,
        out_specs=(P(), frames),
        check_vma=False,
    )
```

```python
import functools

import jax
import jax.numpy as jnp
from jax import lax
from jax.experimental import pallas as pl
from jax.experimental.pallas import tpu as pltpu
from jax.sharding import PartitionSpec as P

MESH = pl.DeviceIdType.MESH
F32 = jnp.float32
BF = jnp.bfloat16
EPS = 1e-06
ROOT = 0.7978845608028654
CUBE = 0.044715

ROWS = 8
NZ = 8
NY = 4


def dot(a, b):
    return lax.dot_general(a, b, (((1,), (0,)), ((), ())), preferred_element_type=F32)


def dot_t(a, b):
    return lax.dot_general(a, b, (((1,), (1,)), ((), ())), preferred_element_type=F32)


def iota(shape, dim):
    return lax.broadcasted_iota(jnp.int32, shape, dim)


def onehot(cond):
    return jnp.where(cond, 1.0, 0.0).astype(BF)


def rounded(x):
    return x.astype(BF).astype(F32)


def gelu(x):
    t = jnp.tanh(x * (ROOT + (ROOT * CUBE) * (x * x)))
    return x * (0.5 + 0.5 * t)


def gelu_both(x):
    x2 = x * x
    t = jnp.tanh(x * (ROOT + (ROOT * CUBE) * x2))
    h = 0.5 + 0.5 * t
    slope = h + (0.5 * x) * (1.0 - t * t) * (ROOT + (3.0 * ROOT * CUBE) * x2)
    return x * h, slope


def tap(r, f, lin, total):
    a = lax.rsqrt(total(r * r) + EPS)
    b = lax.rsqrt(total(f * f) + EPS)
    nf = f * b
    d = r * a - nf
    ld = lin * d
    grad = (ld - nf * total(nf * ld)) * (-2.0 * b)
    return ld * d, grad


def lane_sum(x):
    return jnp.sum(x, axis=-1, keepdims=True)


def fold(x):
    m, c = x.shape
    y = jnp.sum(x.reshape(m // 8, 8, c), axis=0)
    out = y[:, 0:128]
    for j in range(1, c // 128):
        out = out + y[:, j * 128 : (j + 1) * 128]
    return out


def shifted(v, phases):
    c = v.shape[-1]
    q = iota((16, c), 0)
    n = phases * 16
    tail = jnp.where(q < 15, pltpu.roll(v[0:16], 15, 0), 0.0)
    head = jnp.where(q > 0, pltpu.roll(v[n - 16 : n], 1, 0), 0.0)
    if phases == 1:
        return head, tail
    left = jnp.concatenate([head, v[0 : n - 16]], axis=0)
    right = jnp.concatenate([v[16:n], tail], axis=0)
    return left, right


def pool_cols(v, phases):
    c = v.shape[-1]
    return jnp.sum(v.reshape(phases // 2, 2, 16, c), axis=1).reshape(phases * 8, c)


def spread_cols(v, phases):
    c = v.shape[-1]
    y = jnp.broadcast_to(v.reshape(phases, 1, 16, c), (phases, 2, 16, c))
    return y.reshape(phases * 32, c)


def body(
    real_ref, fake_ref, w1_ref, w2_hbm, w3_hbm, w4_hbm, w5_hbm,
    b1_ref, b2_ref, b3_ref, b4_ref, b5_ref, l1_ref, l2_ref, l3_ref, l4_ref, l5_ref,
    loss_ref, grad_ref,
    w2s, w2t, w3s, w4s, w5s, wsm, wb, vec, tt,
    x2, x3, x4, x5, g2, g3, g4, g5, gp1,
    act1, sl1, act2, sl2, act3, sl3,
    a1, s1, a2, s2, a3, s3, a4, s4,
    stage0, land0, stage5, land5, stage4, land4,
    parts, own, lrow, lz, ly,
    wsem, ssem, rsem, gsend, grecv, lsend, lrecv,
):
    dp = lax.axis_index("dp")
    me = lax.axis_index("rows")
    zi = lax.rem(dp, NZ)
    yi = lax.div(dp, NZ)
    not_first = me > 0
    not_last = me < ROWS - 1

    def row_peer(k):
        return (dp, lax.rem(me + k, ROWS))

    def z_peer(k):
        return (yi * NZ + lax.rem(zi + k, NZ), me)

    def y_peer(k):
        return (lax.rem(yi + k, NY) * NZ + zi, me)

    cw2 = [
        pltpu.make_async_copy(
            w2_hbm.at[pl.ds(ky * 192, 192)], w2s.at[ky, pl.ds(0, 192)], wsem.at[ky]
        )
        for ky in range(3)
    ]
    cw3 = pltpu.make_async_copy(w3_hbm, w3s, wsem.at[3])
    cw4 = pltpu.make_async_copy(w4_hbm, w4s, wsem.at[4])
    cw5 = pltpu.make_async_copy(w5_hbm, w5s, wsem.at[5])
    for c in cw2 + [cw3, cw4, cw5]:
        c.start()

    barrier = pltpu.get_barrier_semaphore()
    peers = (
        [row_peer(k) for k in range(1, ROWS)]
        + [z_peer(k) for k in range(1, NZ)]
        + [y_peer(k) for k in range(1, NY)]
    )
    for peer in peers:
        pl.semaphore_signal(barrier, inc=1, device_id=peer, device_id_type=MESH)

    def beside(first, second, land, n):
        up = pltpu.make_async_remote_copy(
            src_ref=first, dst_ref=land.at[1], send_sem=ssem.at[n, 0],
            recv_sem=rsem.at[n, 1], device_id=row_peer(ROWS - 1), device_id_type=MESH,
        )
        down = pltpu.make_async_remote_copy(
            src_ref=second, dst_ref=land.at[0], send_sem=ssem.at[n, 1],
            recv_sem=rsem.at[n, 0], device_id=row_peer(1), device_id_type=MESH,
        )
        return up, down

    stage0[0:48] = real_ref[0].reshape(48, 256)
    stage0[48:96] = fake_ref[0].reshape(48, 256)

    wsm[...] = jnp.zeros_like(wsm)
    for ky in range(3):
        for kx in range(3):
            piece = w1_ref[ky, kx].astype(F32)
            for p in range(2):
                lane = (kx + p) * 128 + p * 64
                wsm[ky * 3 : ky * 3 + 3, lane : lane + 64] = piece
    small = wsm[...].astype(BF)

    for k in range(9):
        idx = iota((64, 16), 0)
        n = iota((64, 16), 1)
        ky = jnp.where(n >= 3, 1, 0) + jnp.where(n >= 6, 1, 0)
        ci = n - 3 * ky
        for half in range(2):
            row = 2 * k + half if k < 8 else 17 * half - 1
            at = row + ky - 1
            inner = (idx >> 4 == ci) & ((idx & 15) == at) & (idx < 48)
            above = (idx - 48 == ci) & (at == -1)
            below = (idx - 51 == ci) & (at == 16)
            block = dot(onehot((inner | above | below) & (n < 9)), small).astype(BF)
            for d in range(4):
                wb[k, d * 64 : (d + 1) * 64, half * 128 : (half + 1) * 128] = block[
                    :, d * 128 : (d + 1) * 128
                ]

    for row, ref in ((0, b1_ref), (1, l1_ref)):
        for q in range(4):
            vec[row : row + 1, q * 64 : (q + 1) * 64] = ref[...]
    ones_part = onehot(iota((256, 256), 0) >> 6 == iota((256, 256), 1) >> 6)
    ones_full = jnp.full((128, 128), 1.0, BF)

    def sum_part(x):
        return dot(x.astype(BF), ones_part)

    def sum_full(x):
        return dot(x.astype(BF), ones_full)

    parts[...] = jnp.zeros_like(parts)
    w2s[:, 192:256, :] = jnp.zeros((3, 64, 128), BF)

    pos = iota((128, 256), 0)
    col = iota((128, 256), 1)
    base = 16 * (pos & 15) + 2 * (pos >> 4)
    take = onehot(col == base)

    def patches(slot, images, sources):
        for i in range(2):
            halo = jnp.zeros((16, 256), F32)
            for source, row, off, ok in sources:
                j = iota((16, 96), 0) - off
                k = iota((16, 96), 1)
                pick = (j >= 0) & (j < 3) & (k == i * 48 + j * 16 + row)
                if ok is not None:
                    pick = pick & ok
                halo = halo + dot(onehot(pick), source)
            whole = jnp.concatenate([images[i * 48 : (i + 1) * 48].astype(F32), halo], axis=0)
            cols = iota((64, 256), 1)
            turned = []
            for d in range(4):
                dx = d - 1
                moved = whole if dx == 0 else pltpu.roll(whole, (-dx) % 256, 1)
                moved = jnp.where((cols + dx >= 0) & (cols + dx < 256), moved, 0.0)
                turned.append(moved.astype(BF))
            tt[slot, i * 128 : (i + 1) * 128, :] = dot_t(
                take, jnp.concatenate(turned, axis=0)
            ).astype(BF)

    mine = stage0[...]
    patches(0, mine, ())

    pl.semaphore_wait(barrier, len(peers))
    c0 = beside(stage0, stage0, land0, 0)
    for c in c0:
        c.start()

    lane = iota((128, 128), 1)
    bias1 = vec[0:1, :]
    lin1 = vec[1:2, :]

    def put2(row, v):
        for i in range(2):
            w = v[i * 128 : (i + 1) * 128]
            left, right = shifted(w, 8)
            x2[row, i * 128 : (i + 1) * 128, 0:128] = jnp.where(lane < 64, left, w).astype(BF)
            x2[row, i * 128 : (i + 1) * 128, 128:256] = right.astype(BF)

    def segment1(slot, k, p, keep, ok):
        pre = dot(tt[slot], wb[k]) + bias1
        if keep is None:
            act = rounded(gelu(pre))
        else:
            act_f, slope = gelu_both(pre[128:256])
            act = rounded(jnp.concatenate([gelu(pre[0:128]), act_f], axis=0))
            if keep == "left":
                act1[8, :, 0:128] = act[:, 128:256].astype(BF)
                sl1[8, :, 0:128] = slope[:, 128:256]
            elif keep == "right":
                act1[8, :, 128:256] = act[:, 0:128].astype(BF)
                sl1[8, :, 128:256] = slope[:, 0:128]
            else:
                act1[k] = act.astype(BF)
                sl1[k] = slope
        s = act[:, 0:128] + act[:, 128:256]
        v = rounded((s + pltpu.roll(s, 64, 1)) * 0.25)
        if ok is not None:
            v = jnp.where(ok, v, 0.0)
        put2(p, v)

    def tap1(k, counted):
        act = act1[k].astype(F32)
        terms, grad = tap(act[0:128], act[128:256], lin1, sum_part)
        if counted:
            parts[0] += fold(terms)
        slope = sl1[k]
        a1[k] = slope * grad
        s1[k] = slope * 0.25

    for k in range(1, 7):
        segment1(0, k, 7 + k, "own", None)
    for k in range(1, 7):
        tap1(k, True)

    for c in cw2:
        c.wait()
    for ky in range(3):
        for kx in range(3):
            piece = w2s[ky, kx * 64 : (kx + 1) * 64, :]
            w2t[ky, 0:64, kx * 128 : (kx + 1) * 128] = piece
            w2t[ky, 64:128, kx * 128 : (kx + 1) * 128] = piece

    for c in c0:
        c.wait()
    upper = land0[0]
    lower = land0[1]
    patches(1, mine, ((upper, 15, 0, not_first), (lower, 0, 3, not_last)))
    patches(2, upper, ((mine, 0, 3, None),))
    patches(3, lower, ((mine, 15, 0, None),))
    segment1(2, 7, 6, "left", not_first)
    segment1(1, 0, 7, "own", None)
    segment1(1, 7, 14, "own", None)
    segment1(3, 0, 15, "right", not_last)

    for k in range(1, 7):
        segment1(2, k, k - 1, None, not_first)
        segment1(3, k, 15 + k, None, not_last)

    def put(ref, row, v, phases, c):
        n = phases * 16
        for i in range(2):
            w = v[i * n : (i + 1) * n]
            left, right = shifted(w, phases)
            ref[row, i * n : (i + 1) * n, 0:c] = left.astype(BF)
            ref[row, i * n : (i + 1) * n, c : 2 * c] = w.astype(BF)
            ref[row, i * n : (i + 1) * n, 2 * c : 3 * c] = right.astype(BF)

    def both(pre, n):
        parts_of = []
        slopes = []
        for row in range(2):
            top = 2 * row * n
            parts_of.append(gelu(pre[top : top + n]))
            act, slope = gelu_both(pre[top + n : top + 2 * n])
            parts_of.append(act)
            slopes.append(slope)
        return rounded(jnp.concatenate(parts_of, axis=0)), jnp.concatenate(slopes, axis=0)

    def segment2(m):
        pre = b2_ref[...]
        for ky in range(3):
            rows = x2[2 * m + ky : 2 * m + ky + 2].reshape(512, 256)
            pre = pre + dot(rows, w2s[ky])
        if 2 <= m < 8:
            act, slope = both(pre, 128)
            act2[m - 2] = act.astype(BF)
            sl2[m - 2] = slope
        else:
            act = rounded(gelu(pre))
        v = rounded(pool_cols(act[0:256] + act[256:512], 16) * 0.25)
        if m < 3:
            v = jnp.where(not_first, v, 0.0)
        if m >= 7:
            v = jnp.where(not_last, v, 0.0)
        put(x3, m, v, 4, 128)

    for m in range(10):
        segment2(m)

    cw3.wait()

    def segment3(n):
        pre = b3_ref[...]
        for ky in range(3):
            rows = x3[2 * n + ky : 2 * n + ky + 2].reshape(256, 384)
            pre = pre + dot(rows, w3s[ky * 384 : (ky + 1) * 384, :])
        act, slope = both(pre, 64)
        act3[n] = act.astype(BF)
        sl3[n] = slope
        v = rounded(pool_cols(act[0:128] + act[128:256], 8) * 0.25)
        if n < 1:
            v = jnp.where(not_first, v, 0.0)
        if n >= 3:
            v = jnp.where(not_last, v, 0.0)
        put(x4, n, v, 2, 256)

    for n in range(4):
        segment3(n)

    cw4.wait()
    pre = b4_ref[...]
    for ky in range(3):
        rows = x4[ky : ky + 2].reshape(128, 768)
        pre = pre + dot(rows, w4s[ky * 768 : (ky + 1) * 768, :])
    act, slope = both(pre, 32)
    stage5[...] = (pool_cols(act[0:64] + act[64:128], 4) * 0.25).astype(BF)
    c5 = [
        pltpu.make_async_remote_copy(
            src_ref=stage5, dst_ref=land5.at[me], send_sem=gsend.at[k - 1],
            recv_sem=grecv.at[k - 1], device_id=row_peer(k), device_id_type=MESH,
        )
        for k in range(1, ROWS)
    ]
    for c in c5:
        c.start()
    land5[me] = stage5[...]

    act = act.reshape(2, 2, 32, 512)
    terms, grad = tap(
        act[:, 0].reshape(64, 512), act[:, 1].reshape(64, 512), l4_ref[...], lane_sum
    )
    parts[3] += fold(terms)
    a = slope * (64.0 * grad)
    s = slope * 0.25
    a4[...] = a.reshape(2, 32, 512)
    s4[...] = s.reshape(2, 32, 512)
    stage4[0:2] = a.astype(BF).reshape(2, 32, 512)
    stage4[2:4] = s.astype(BF).reshape(2, 32, 512)
    c4 = beside(stage4, stage4, land4, 1)
    for c in c4:
        c.start()

    def tap3(n, counted):
        act = act3[n].astype(F32).reshape(2, 2, 64, 256)
        slope = sl3[n]
        terms, grad = tap(
            act[:, 0].reshape(128, 256), act[:, 1].reshape(128, 256), l3_ref[...], lane_sum
        )
        if counted:
            parts[2] += fold(terms)
        a3[2 * n : 2 * n + 2] = (slope * (16.0 * grad)).reshape(2, 64, 256)
        s3[2 * n : 2 * n + 2] = (slope * 0.25).reshape(2, 64, 256)

    def tap2(m, counted):
        act = act2[m - 2].astype(F32).reshape(2, 2, 128, 128)
        slope = sl2[m - 2]
        terms, grad = tap(
            act[:, 0].reshape(256, 128), act[:, 1].reshape(256, 128), l2_ref[...], sum_full
        )
        if counted:
            parts[1] += fold(terms)
        a2[2 * m - 4 : 2 * m - 2] = (slope * (4.0 * grad)).reshape(2, 128, 128)
        s2[2 * m - 4 : 2 * m - 2] = (slope * 0.25).reshape(2, 128, 128)

    tap1(0, True)
    tap1(7, True)
    tap1(8, False)
    tap3(1, True)
    tap3(2, True)

    for m in range(3, 7):
        tap2(m, True)

    def spread_loss(src, land, slot, peer, count, first):
        copies = [
            pltpu.make_async_remote_copy(
                src_ref=src, dst_ref=land.at[slot], send_sem=lsend.at[first + k],
                recv_sem=lrecv.at[first + k], device_id=peer(k), device_id_type=MESH,
            )
            for k in range(1, count)
        ]
        for c in copies:
            c.start()
        land[slot] = src[...]
        return copies

    def gathered_loss(copies, land, count):
        for c in copies:
            c.wait()
        total = land[0]
        for j in range(1, count):
            total = total + land[j]
        return total

    rows_of = iota((8, 128), 0)
    sums = jnp.zeros((8, 128), F32)
    for s in range(4):
        sums = sums + jnp.where(rows_of == s, jnp.sum(parts[s], axis=0, keepdims=True), 0.0)
    own[0] = sums
    cl = spread_loss(own.at[0], lrow, me, row_peer, ROWS, 0)

    tap2(2, False)
    tap2(7, False)
    tap3(0, False)
    tap3(3, False)

    for row in (0, 9):
        x5[row] = jnp.zeros((32, 1536), BF)
    for row in (0, 1, 10, 11):
        g5[row] = jnp.zeros((16, 1536), BF)
    cw5.wait()
    for c in c5:
        c.wait()
    for row in range(ROWS):
        put(x5, row + 1, land5[row].astype(F32), 1, 512)
    pre = b5_ref[...]
    for ky in range(3):
        rows = x5[ky : ky + 8].reshape(256, 1536)
        pre = pre + dot(rows, w5s[ky * 1536 : (ky + 1) * 1536, :])
    pre = pre.reshape(8, 2, 16, 512)
    act_r = rounded(gelu(pre[:, 0].reshape(128, 512)))
    act_f, slope = gelu_both(pre[:, 1].reshape(128, 512))
    act_f = rounded(act_f)
    terms, grad = tap(act_r, act_f, l5_ref[...], lane_sum)
    gpre = rounded(slope * (256.0 * grad))

    def put_back(ref, row, v, phases, c):
        left, right = shifted(v, phases)
        ref[row, :, 0:c] = right.astype(BF)
        ref[row, :, c : 2 * c] = v.astype(BF)
        ref[row, :, 2 * c : 3 * c] = left.astype(BF)

    for row in range(ROWS):
        put_back(g5, row + 2, gpre[row * 16 : (row + 1) * 16], 1, 512)
    fifth = jnp.sum(fold(terms), axis=0, keepdims=True)
    own[1] = gathered_loss(cl, lrow, ROWS) + jnp.where(rows_of == 4, fifth, 0.0)
    cl = spread_loss(own.at[1], lz, zi, z_peer, NZ, 8)

    gin = jnp.zeros((48, 512), F32)
    for ky in range(3):
        rows = g5[pl.ds(me + 2 - ky, 3)].reshape(48, 1536)
        for kx in range(3):
            n = (ky * 3 + kx) * 512
            gin = gin + dot_t(rows[:, kx * 512 : (kx + 1) * 512], w5s[n : n + 512, :])

    for c in c4:
        c.wait()
    for u in range(6):
        wide = spread_cols(gin[(u // 2) * 16 : (u // 2 + 1) * 16], 1)
        if 2 <= u < 4:
            v = a4[u - 2] + s4[u - 2] * wide
        else:
            side, j, ok = (0, u, not_first) if u < 2 else (1, u - 4, not_last)
            a = land4[side, j].astype(F32)
            s = land4[side, 2 + j].astype(F32)
            v = jnp.where(ok, a + s * wide, 0.0)
        put_back(g4, u, rounded(v), 2, 512)
    gin = jnp.zeros((128, 256), F32)
    for ky in range(3):
        rows = g4[2 - ky : 6 - ky].reshape(128, 1536)
        for kx in range(3):
            n = (ky * 3 + kx) * 256
            gin = gin + dot_t(rows[:, kx * 512 : (kx + 1) * 512], w4s[n : n + 256, :])

    for j in range(8):
        wide = spread_cols(gin[(j // 2) * 32 : (j // 2 + 1) * 32], 2)
        v = a3[j] + s3[j] * wide
        if j < 2:
            v = jnp.where(not_first, v, 0.0)
        if j >= 6:
            v = jnp.where(not_last, v, 0.0)
        put_back(g3, j, rounded(v), 4, 256)
    gin = 0.0
    for ky in range(3):
        rows = g3[2 - ky : 8 - ky].reshape(384, 768)
        for kx in range(3):
            n = (ky * 3 + kx) * 128
            gin = gin + dot_t(rows[:, kx * 256 : (kx + 1) * 256], w3s[n : n + 128, :])
    own[2] = gathered_loss(cl, lz, NZ)
    cl = spread_loss(own.at[2], ly, yi, y_peer, NY, 16)

    for j in range(12):
        wide = spread_cols(gin[(j // 2) * 64 : (j // 2 + 1) * 64], 4)
        v = a2[j] + s2[j] * wide
        if j < 2:
            v = jnp.where(not_first, v, 0.0)
        if j >= 10:
            v = jnp.where(not_last, v, 0.0)
        put_back(g2, j, rounded(v), 8, 128)

    for n in range(4):
        g = 0.0
        for ky in range(3):
            rows = g2[2 * n + 3 - ky : 2 * n + 5 - ky].reshape(256, 384)
            g = g + dot_t(rows, w2t[ky])
        for j in range(2):
            k = 2 * n + j
            one = g[j * 128 : (j + 1) * 128]
            wide = jnp.concatenate([one, one], axis=1)
            gp1[k] = (a1[k] + s1[k] * wide).astype(BF)
    g = 0.0
    for ky in range(3):
        rows = jnp.concatenate([g2[2 - ky], g2[11 - ky]], axis=0)
        g = g + dot_t(rows, w2t[ky])
    above = jnp.where(not_first, a1[8, :, 0:128] + s1[8, :, 0:128] * g[0:128], 0.0)
    below = jnp.where(not_last, a1[8, :, 128:256] + s1[8, :, 128:256] * g[128:256], 0.0)
    gp1[8] = jnp.concatenate([above, below], axis=1).astype(BF)

    g = jnp.zeros((128, 256), F32)
    for k in range(9):
        g = g + dot_t(gp1[k], wb[k])
    across = jnp.transpose(g)
    lined = jnp.concatenate([across[d * 64 : (d + 1) * 64] for d in range(4)], axis=1)
    back = jnp.concatenate([onehot(col == base + d - 1) for d in range(4)], axis=0)
    high = lined.astype(BF)
    low = (lined - high.astype(F32)).astype(BF)
    out = dot(high, back) + dot(low, back)
    grad_ref[0] = out[0:48].reshape(3, 16, 256)

    total = gathered_loss(cl, ly, NY)
    sums = jnp.sum(total, axis=1, keepdims=True)
    lanes = iota((8, 128), 1)
    counts = [32.0 * (128 >> s) * (256 >> s) for s in range(5)]
    scale = jnp.zeros((8, 128), F32)
    for s in range(5):
        scale = scale + jnp.where((lanes == s) & (rows_of == s), 1.0 / counts[s], 0.0)
    loss_ref[...] = jnp.sum(sums * scale, axis=0, keepdims=True)[:, 0:5]


def hand_on(losses_ref, grads_ref, loss_ref, grad_ref):
    loss_ref[...] = losses_ref[...]
    grad_ref[...] = grads_ref[...]


def on_device(*args):
    (real, fake, w1, w2, w3, w4, w5, *vectors) = args
    flat = [w.reshape(-1, w.shape[-1]) for w in (w2, w3, w4, w5)]
    vectors = [v.reshape(1, -1) for v in vectors]
    vmem = pl.BlockSpec(memory_space=pltpu.VMEM)
    anywhere = pl.BlockSpec(memory_space=pl.ANY)
    v = pltpu.VMEM
    dma = pltpu.SemaphoreType.DMA
    scratch = [
        v((3, 256, 128), BF), v((3, 128, 384), BF), v((1152, 256), BF), v((2304, 512), BF),
        v((4608, 512), BF), v((16, 512), F32), v((9, 256, 256), BF), v((8, 256), F32),
        v((4, 256, 256), BF),
        v((22, 256, 256), BF), v((10, 128, 384), BF), v((4, 64, 768), BF), v((10, 32, 1536), BF),
        v((12, 128, 384), BF), v((8, 64, 768), BF), v((6, 32, 1536), BF), v((12, 16, 1536), BF),
        v((9, 128, 256), BF),
        v((9, 256, 256), BF), v((9, 128, 256), F32), v((6, 512, 128), BF),
        v((6, 256, 128), F32), v((4, 256, 256), BF), v((4, 128, 256), F32),
        v((9, 128, 256), F32), v((9, 128, 256), F32), v((12, 128, 128), F32),
        v((12, 128, 128), F32), v((8, 64, 256), F32), v((8, 64, 256), F32),
        v((2, 32, 512), F32), v((2, 32, 512), F32),
        v((96, 256), BF), v((2, 96, 256), BF), v((32, 512), BF), v((8, 32, 512), BF),
        v((4, 32, 512), BF), v((2, 4, 32, 512), BF),
        v((5, 8, 128), F32), v((3, 8, 128), F32), v((8, 8, 128), F32), v((8, 8, 128), F32),
        v((4, 8, 128), F32),
        dma((6,)), dma((2, 2)), dma((2, 2)), dma((7,)), dma((7,)), dma((24,)), dma((24,)),
    ]
    losses, grads = pl.pallas_call(
        body,
        out_shape=(
            jax.ShapeDtypeStruct((1, 5), F32),
            jax.ShapeDtypeStruct((1, 3, 16, 256), F32),
        ),
        in_specs=[vmem] * 3 + [anywhere] * 4 + [vmem] * 10,
        out_specs=(vmem, vmem),
        scratch_shapes=scratch,
        compiler_params=pltpu.CompilerParams(
            collective_id=0, has_side_effects=True, vmem_limit_bytes=56 << 20
        ),
        name="whole_step",
    )(real, fake, w1, *flat, *vectors)
    losses, grads = pl.pallas_call(
        hand_on,
        out_shape=(
            jax.ShapeDtypeStruct((1, 5), F32),
            jax.ShapeDtypeStruct((1, 3, 16, 256), F32),
        ),
        in_specs=[vmem] * 2,
        out_specs=(vmem, vmem),
        name="hand_on",
    )(losses, grads)
    return (losses.reshape(5), grads)


def solution(mesh):
    frames = P("dp", None, "rows", None)
    return jax.shard_map(
        on_device,
        mesh=mesh,
        in_specs=(frames, frames) + (P(),) * 15,
        out_specs=(P(), frames),
        check_vma=False,
    )
```

```python
import functools

import jax
import jax.numpy as jnp
from jax import lax
from jax.experimental import pallas as pl
from jax.experimental.pallas import tpu as pltpu
from jax.sharding import PartitionSpec as P

MESH = pl.DeviceIdType.MESH
F32 = jnp.float32
BF = jnp.bfloat16
EPS = 1e-06
ROOT = 0.7978845608028654
CUBE = 0.044715

ROWS = 8
DP = 32


def dot(a, b):
    return lax.dot_general(a, b, (((1,), (0,)), ((), ())), preferred_element_type=F32)


def dot_t(a, b):
    return lax.dot_general(a, b, (((1,), (1,)), ((), ())), preferred_element_type=F32)


def iota(shape, dim):
    return lax.broadcasted_iota(jnp.int32, shape, dim)


def onehot(cond):
    return jnp.where(cond, 1.0, 0.0).astype(BF)


def rounded(x):
    return x.astype(BF).astype(F32)


def gelu(x):
    t = jnp.tanh(x * (ROOT + (ROOT * CUBE) * (x * x)))
    return x * (0.5 + 0.5 * t)


def gelu_both(x):
    x2 = x * x
    t = jnp.tanh(x * (ROOT + (ROOT * CUBE) * x2))
    h = 0.5 + 0.5 * t
    slope = h + (0.5 * x) * (1.0 - t * t) * (ROOT + (3.0 * ROOT * CUBE) * x2)
    return x * h, slope


def tap(r, f, lin, total):
    a = lax.rsqrt(total(r * r) + EPS)
    b = lax.rsqrt(total(f * f) + EPS)
    nf = f * b
    d = r * a - nf
    ld = lin * d
    grad = (ld - nf * total(nf * ld)) * (-2.0 * b)
    return ld * d, grad


def lane_sum(x):
    return jnp.sum(x, axis=-1, keepdims=True)


def fold(x):
    m, c = x.shape
    y = jnp.sum(x.reshape(m // 8, 8, c), axis=0)
    out = y[:, 0:128]
    for j in range(1, c // 128):
        out = out + y[:, j * 128 : (j + 1) * 128]
    return out


def shifted(v, phases):
    c = v.shape[-1]
    q = iota((16, c), 0)
    n = phases * 16
    tail = jnp.where(q < 15, pltpu.roll(v[0:16], 15, 0), 0.0)
    head = jnp.where(q > 0, pltpu.roll(v[n - 16 : n], 1, 0), 0.0)
    if phases == 1:
        return head, tail
    left = jnp.concatenate([head, v[0 : n - 16]], axis=0)
    right = jnp.concatenate([v[16:n], tail], axis=0)
    return left, right


def pool_cols(v, phases):
    c = v.shape[-1]
    return jnp.sum(v.reshape(phases // 2, 2, 16, c), axis=1).reshape(phases * 8, c)


def spread_cols(v, phases):
    c = v.shape[-1]
    y = jnp.broadcast_to(v.reshape(phases, 1, 16, c), (phases, 2, 16, c))
    return y.reshape(phases * 32, c)


def body(
    real_ref, fake_ref, w1_ref, w2_hbm, w3_hbm, w4_hbm, w5_hbm,
    b1_ref, b2_ref, b3_ref, b4_ref, b5_ref, l1_ref, l2_ref, l3_ref, l4_ref, l5_ref,
    loss_ref, grad_ref,
    w2s, w2t, w3s, w4s, w5s, wsm, wb, vec, tt,
    x2, x3, x4, x5, g2, g3, g4, g5, gp1,
    act1, sl1, act2, sl2, act3, sl3,
    a1, s1, a2, s2, a3, s3, a4, s4,
    stage0, land0, stage5, land5, stage4, land4,
    parts, own, lrow, lall,
    wsem, ssem, rsem, gsend, grecv, lsend, lrecv,
):
    dp = lax.axis_index("dp")
    me = lax.axis_index("rows")
    not_first = me > 0
    not_last = me < ROWS - 1

    def row_peer(k):
        return (dp, lax.rem(me + k, ROWS))

    def dp_peer(k):
        return (lax.rem(dp + k, DP), me)

    cw2 = [
        pltpu.make_async_copy(
            w2_hbm.at[pl.ds(ky * 192, 192)], w2s.at[ky, pl.ds(0, 192)], wsem.at[ky]
        )
        for ky in range(3)
    ]
    cw3 = pltpu.make_async_copy(w3_hbm, w3s, wsem.at[3])
    cw4 = pltpu.make_async_copy(w4_hbm, w4s, wsem.at[4])
    cw5 = pltpu.make_async_copy(w5_hbm, w5s, wsem.at[5])
    for c in cw2 + [cw3, cw4, cw5]:
        c.start()

    barrier = pltpu.get_barrier_semaphore()
    peers = [row_peer(k) for k in range(1, ROWS)] + [dp_peer(k) for k in range(1, DP)]
    for peer in peers:
        pl.semaphore_signal(barrier, inc=1, device_id=peer, device_id_type=MESH)

    def beside(first, second, land, n):
        up = pltpu.make_async_remote_copy(
            src_ref=first, dst_ref=land.at[1], send_sem=ssem.at[n, 0],
            recv_sem=rsem.at[n, 1], device_id=row_peer(ROWS - 1), device_id_type=MESH,
        )
        down = pltpu.make_async_remote_copy(
            src_ref=second, dst_ref=land.at[0], send_sem=ssem.at[n, 1],
            recv_sem=rsem.at[n, 0], device_id=row_peer(1), device_id_type=MESH,
        )
        return up, down

    stage0[0:48] = real_ref[0].reshape(48, 256)
    stage0[48:96] = fake_ref[0].reshape(48, 256)

    wsm[...] = jnp.zeros_like(wsm)
    for ky in range(3):
        for kx in range(3):
            piece = w1_ref[ky, kx].astype(F32)
            for p in range(2):
                lane = (kx + p) * 128 + p * 64
                wsm[ky * 3 : ky * 3 + 3, lane : lane + 64] = piece
    small = wsm[...].astype(BF)

    for k in range(9):
        idx = iota((64, 16), 0)
        n = iota((64, 16), 1)
        ky = jnp.where(n >= 3, 1, 0) + jnp.where(n >= 6, 1, 0)
        ci = n - 3 * ky
        for half in range(2):
            row = 2 * k + half if k < 8 else 17 * half - 1
            at = row + ky - 1
            inner = (idx >> 4 == ci) & ((idx & 15) == at) & (idx < 48)
            above = (idx - 48 == ci) & (at == -1)
            below = (idx - 51 == ci) & (at == 16)
            block = dot(onehot((inner | above | below) & (n < 9)), small).astype(BF)
            for d in range(4):
                wb[k, d * 64 : (d + 1) * 64, half * 128 : (half + 1) * 128] = block[
                    :, d * 128 : (d + 1) * 128
                ]

    for row, ref in ((0, b1_ref), (1, l1_ref)):
        for q in range(4):
            vec[row : row + 1, q * 64 : (q + 1) * 64] = ref[...]
    ones_part = onehot(iota((256, 256), 0) >> 6 == iota((256, 256), 1) >> 6)
    ones_full = jnp.full((128, 128), 1.0, BF)

    def sum_part(x):
        return dot(x.astype(BF), ones_part)

    def sum_full(x):
        return dot(x.astype(BF), ones_full)

    parts[...] = jnp.zeros_like(parts)
    w2s[:, 192:256, :] = jnp.zeros((3, 64, 128), BF)

    pos = iota((128, 256), 0)
    col = iota((128, 256), 1)
    base = 16 * (pos & 15) + 2 * (pos >> 4)
    take = onehot(col == base)

    def patches(slot, images, sources):
        for i in range(2):
            halo = jnp.zeros((16, 256), F32)
            for source, row, off, ok in sources:
                j = iota((16, 96), 0) - off
                k = iota((16, 96), 1)
                pick = (j >= 0) & (j < 3) & (k == i * 48 + j * 16 + row)
                if ok is not None:
                    pick = pick & ok
                halo = halo + dot(onehot(pick), source)
            whole = jnp.concatenate([images[i * 48 : (i + 1) * 48].astype(F32), halo], axis=0)
            cols = iota((64, 256), 1)
            turned = []
            for d in range(4):
                dx = d - 1
                moved = whole if dx == 0 else pltpu.roll(whole, (-dx) % 256, 1)
                moved = jnp.where((cols + dx >= 0) & (cols + dx < 256), moved, 0.0)
                turned.append(moved.astype(BF))
            tt[slot, i * 128 : (i + 1) * 128, :] = dot_t(
                take, jnp.concatenate(turned, axis=0)
            ).astype(BF)

    mine = stage0[...]
    patches(0, mine, ())

    lane = iota((128, 128), 1)
    bias1 = vec[0:1, :]
    lin1 = vec[1:2, :]

    def put2(row, v):
        for i in range(2):
            w = v[i * 128 : (i + 1) * 128]
            left, right = shifted(w, 8)
            x2[row, i * 128 : (i + 1) * 128, 0:128] = jnp.where(lane < 64, left, w).astype(BF)
            x2[row, i * 128 : (i + 1) * 128, 128:256] = right.astype(BF)

    def segment1(slot, k, p, keep, ok):
        pre = dot(tt[slot], wb[k]) + bias1
        if keep is None:
            act = rounded(gelu(pre))
        else:
            act_f, slope = gelu_both(pre[128:256])
            act = rounded(jnp.concatenate([gelu(pre[0:128]), act_f], axis=0))
            act1[keep] = act.astype(BF)
            sl1[keep] = slope
        s = act[:, 0:128] + act[:, 128:256]
        v = rounded((s + pltpu.roll(s, 64, 1)) * 0.25)
        if ok is not None:
            v = jnp.where(ok, v, 0.0)
        put2(p, v)

    def tap1(k, counted):
        act = act1[k].astype(F32)
        slope = sl1[k]
        if k == 8:
            act = jnp.concatenate([act[:, 128:256], act1[9, :, 0:128].astype(F32)], axis=1)
            slope = jnp.concatenate([slope[:, 128:256], sl1[9, :, 0:128]], axis=1)
        terms, grad = tap(act[0:128], act[128:256], lin1, sum_part)
        if counted:
            parts[0] += fold(terms)
        a1[k] = slope * grad
        s1[k] = slope * 0.25

    for k in range(1, 7):
        segment1(0, k, 7 + k, k, None)

    pl.semaphore_wait(barrier, len(peers))
    c0 = beside(stage0, stage0, land0, 0)
    for c in c0:
        c.start()
    for k in range(1, 5):
        tap1(k, True)

    for c in cw2:
        c.wait()
    for ky in range(3):
        for kx in range(3):
            piece = w2s[ky, kx * 64 : (kx + 1) * 64, :]
            w2t[ky, 0:64, kx * 128 : (kx + 1) * 128] = piece
            w2t[ky, 64:128, kx * 128 : (kx + 1) * 128] = piece

    def edge1(side, slot):
        pltpu.make_async_remote_copy(
            src_ref=stage0, dst_ref=land0.at[side], send_sem=ssem.at[0, 0],
            recv_sem=rsem.at[0, side], device_id=row_peer(1), device_id_type=MESH,
        ).wait_recv()
        ok = ((side == 0) & not_first) | ((side == 1) & not_last)
        other = land0[side]
        patches(slot, mine, ((other, 15 * (1 - side), 3 * side, ok),))
        patches(slot + 1, other, ((mine, 15 * side, 3 * (1 - side), None),))
        segment1(slot, 7 * side, 7 + 7 * side, 7 * side, None)
        segment1(slot + 1, 7 * (1 - side), 6 + 9 * side, 8 + side, ok)
        for k in range(1, 7):
            segment1(slot + 1, k, k - 1 + 16 * side, None, ok)

    near = 1 - lax.rem(me, 2)
    edge1(near, 1)

    def put(ref, row, v, phases, c):
        n = phases * 16
        for i in range(2):
            w = v[i * n : (i + 1) * n]
            left, right = shifted(w, phases)
            ref[row, i * n : (i + 1) * n, 0:c] = left.astype(BF)
            ref[row, i * n : (i + 1) * n, c : 2 * c] = w.astype(BF)
            ref[row, i * n : (i + 1) * n, 2 * c : 3 * c] = right.astype(BF)

    def both(pre, n):
        parts_of = []
        slopes = []
        for row in range(2):
            top = 2 * row * n
            parts_of.append(gelu(pre[top : top + n]))
            act, slope = gelu_both(pre[top + n : top + 2 * n])
            parts_of.append(act)
            slopes.append(slope)
        return rounded(jnp.concatenate(parts_of, axis=0)), jnp.concatenate(slopes, axis=0)

    def segment2(m):
        pre = b2_ref[...]
        for ky in range(3):
            rows = x2[pl.ds(2 * m + ky, 2)].reshape(512, 256)
            pre = pre + dot(rows, w2s[ky])
        act, slope = both(pre, 128)
        act2[m] = act.astype(BF)
        sl2[m] = slope
        v = rounded(pool_cols(act[0:256] + act[256:512], 16) * 0.25)
        ok = ((m >= 3) | not_first) & ((m < 7) | not_last)
        put(x3, m, jnp.where(ok, v, 0.0), 4, 128)

    for i in range(6):
        segment2(4 * near + i)
    edge1(1 - near, 3)
    for i in range(4):
        segment2(6 * (1 - near) + i)
    for c in c0:
        c.wait_send()

    cw3.wait()

    def segment3(n):
        pre = b3_ref[...]
        for ky in range(3):
            rows = x3[2 * n + ky : 2 * n + ky + 2].reshape(256, 384)
            pre = pre + dot(rows, w3s[ky * 384 : (ky + 1) * 384, :])
        act, slope = both(pre, 64)
        act3[n] = act.astype(BF)
        sl3[n] = slope
        v = rounded(pool_cols(act[0:128] + act[128:256], 8) * 0.25)
        if n < 1:
            v = jnp.where(not_first, v, 0.0)
        if n >= 3:
            v = jnp.where(not_last, v, 0.0)
        put(x4, n, v, 2, 256)

    for n in range(4):
        segment3(n)

    cw4.wait()
    pre = b4_ref[...]
    for ky in range(3):
        rows = x4[ky : ky + 2].reshape(128, 768)
        pre = pre + dot(rows, w4s[ky * 768 : (ky + 1) * 768, :])
    act, slope = both(pre, 32)
    stage5[...] = (pool_cols(act[0:64] + act[64:128], 4) * 0.25).astype(BF)
    c5 = [
        pltpu.make_async_remote_copy(
            src_ref=stage5, dst_ref=land5.at[me], send_sem=gsend.at[k - 1],
            recv_sem=grecv.at[k - 1], device_id=row_peer(k), device_id_type=MESH,
        )
        for k in range(1, ROWS)
    ]
    for c in c5:
        c.start()
    land5[me] = stage5[...]

    act = act.reshape(2, 2, 32, 512)
    terms, grad = tap(
        act[:, 0].reshape(64, 512), act[:, 1].reshape(64, 512), l4_ref[...], lane_sum
    )
    parts[3] += fold(terms)
    a = slope * (64.0 * grad)
    s = slope * 0.25
    a4[...] = a.reshape(2, 32, 512)
    s4[...] = s.reshape(2, 32, 512)
    stage4[0:2] = a.astype(BF).reshape(2, 32, 512)
    stage4[2:4] = s.astype(BF).reshape(2, 32, 512)
    c4 = beside(stage4, stage4, land4, 1)
    for c in c4:
        c.start()

    def tap3(n, counted):
        act = act3[n].astype(F32).reshape(2, 2, 64, 256)
        slope = sl3[n]
        terms, grad = tap(
            act[:, 0].reshape(128, 256), act[:, 1].reshape(128, 256), l3_ref[...], lane_sum
        )
        if counted:
            parts[2] += fold(terms)
        a3[2 * n : 2 * n + 2] = (slope * (16.0 * grad)).reshape(2, 64, 256)
        s3[2 * n : 2 * n + 2] = (slope * 0.25).reshape(2, 64, 256)

    def tap2(m, counted):
        act = act2[m].astype(F32).reshape(2, 2, 128, 128)
        slope = sl2[m]
        terms, grad = tap(
            act[:, 0].reshape(256, 128), act[:, 1].reshape(256, 128), l2_ref[...], sum_full
        )
        if counted:
            parts[1] += fold(terms)
        a2[2 * m - 4 : 2 * m - 2] = (slope * (4.0 * grad)).reshape(2, 128, 128)
        s2[2 * m - 4 : 2 * m - 2] = (slope * 0.25).reshape(2, 128, 128)

    for k in (5, 6, 0, 7):
        tap1(k, True)
    tap1(8, False)
    tap3(1, True)
    tap3(2, True)

    for m in range(3, 7):
        tap2(m, True)

    def spread_loss(src, land, slot, peer, count, first):
        copies = [
            pltpu.make_async_remote_copy(
                src_ref=src, dst_ref=land.at[slot], send_sem=lsend.at[first + k],
                recv_sem=lrecv.at[first + k], device_id=peer(k), device_id_type=MESH,
            )
            for k in range(1, count)
        ]
        for c in copies:
            c.start()
        land[slot] = src[...]
        return copies

    def gathered_loss(copies, land, count):
        for c in copies:
            c.wait()
        total = land[0]
        for j in range(1, count):
            total = total + land[j]
        return total

    rows_of = iota((8, 128), 0)
    sums = jnp.zeros((8, 128), F32)
    for s in range(4):
        sums = sums + jnp.where(rows_of == s, jnp.sum(parts[s], axis=0, keepdims=True), 0.0)
    own[0] = sums
    cl = spread_loss(own.at[0], lrow, me, row_peer, ROWS, 0)

    tap2(2, False)
    tap2(7, False)
    tap3(0, False)
    tap3(3, False)

    for row in (0, 9):
        x5[row] = jnp.zeros((32, 1536), BF)
    for row in (0, 1, 10, 11):
        g5[row] = jnp.zeros((16, 1536), BF)
    cw5.wait()
    for c in c5:
        c.wait()
    for row in range(ROWS):
        put(x5, row + 1, land5[row].astype(F32), 1, 512)
    pre = b5_ref[...]
    for ky in range(3):
        rows = x5[ky : ky + 8].reshape(256, 1536)
        pre = pre + dot(rows, w5s[ky * 1536 : (ky + 1) * 1536, :])
    pre = pre.reshape(8, 2, 16, 512)
    act_r = rounded(gelu(pre[:, 0].reshape(128, 512)))
    act_f, slope = gelu_both(pre[:, 1].reshape(128, 512))
    act_f = rounded(act_f)
    terms, grad = tap(act_r, act_f, l5_ref[...], lane_sum)
    gpre = rounded(slope * (256.0 * grad))

    def put_back(ref, row, v, phases, c):
        left, right = shifted(v, phases)
        ref[row, :, 0:c] = right.astype(BF)
        ref[row, :, c : 2 * c] = v.astype(BF)
        ref[row, :, 2 * c : 3 * c] = left.astype(BF)

    for row in range(ROWS):
        put_back(g5, row + 2, gpre[row * 16 : (row + 1) * 16], 1, 512)
    fifth = jnp.sum(fold(terms), axis=0, keepdims=True)
    own[1] = gathered_loss(cl, lrow, ROWS) + jnp.where(rows_of == 4, fifth, 0.0)
    cl = spread_loss(own.at[1], lall, dp, dp_peer, DP, 8)

    gin = jnp.zeros((48, 512), F32)
    for ky in range(3):
        rows = g5[pl.ds(me + 2 - ky, 3)].reshape(48, 1536)
        for kx in range(3):
            n = (ky * 3 + kx) * 512
            gin = gin + dot_t(rows[:, kx * 512 : (kx + 1) * 512], w5s[n : n + 512, :])

    for c in c4:
        c.wait()
    for u in range(6):
        wide = spread_cols(gin[(u // 2) * 16 : (u // 2 + 1) * 16], 1)
        if 2 <= u < 4:
            v = a4[u - 2] + s4[u - 2] * wide
        else:
            side, j, ok = (0, u, not_first) if u < 2 else (1, u - 4, not_last)
            a = land4[side, j].astype(F32)
            s = land4[side, 2 + j].astype(F32)
            v = jnp.where(ok, a + s * wide, 0.0)
        put_back(g4, u, rounded(v), 2, 512)
    gin = jnp.zeros((128, 256), F32)
    for ky in range(3):
        rows = g4[2 - ky : 6 - ky].reshape(128, 1536)
        for kx in range(3):
            n = (ky * 3 + kx) * 256
            gin = gin + dot_t(rows[:, kx * 512 : (kx + 1) * 512], w4s[n : n + 256, :])

    for j in range(8):
        wide = spread_cols(gin[(j // 2) * 32 : (j // 2 + 1) * 32], 2)
        v = a3[j] + s3[j] * wide
        if j < 2:
            v = jnp.where(not_first, v, 0.0)
        if j >= 6:
            v = jnp.where(not_last, v, 0.0)
        put_back(g3, j, rounded(v), 4, 256)
    gin = 0.0
    for ky in range(3):
        rows = g3[2 - ky : 8 - ky].reshape(384, 768)
        for kx in range(3):
            n = (ky * 3 + kx) * 128
            gin = gin + dot_t(rows[:, kx * 256 : (kx + 1) * 256], w3s[n : n + 128, :])

    for j in range(12):
        wide = spread_cols(gin[(j // 2) * 64 : (j // 2 + 1) * 64], 4)
        v = a2[j] + s2[j] * wide
        if j < 2:
            v = jnp.where(not_first, v, 0.0)
        if j >= 10:
            v = jnp.where(not_last, v, 0.0)
        put_back(g2, j, rounded(v), 8, 128)

    for n in range(4):
        g = 0.0
        for ky in range(3):
            rows = g2[2 * n + 3 - ky : 2 * n + 5 - ky].reshape(256, 384)
            g = g + dot_t(rows, w2t[ky])
        for j in range(2):
            k = 2 * n + j
            one = g[j * 128 : (j + 1) * 128]
            wide = jnp.concatenate([one, one], axis=1)
            gp1[k] = (a1[k] + s1[k] * wide).astype(BF)
    g = 0.0
    for ky in range(3):
        rows = jnp.concatenate([g2[2 - ky], g2[11 - ky]], axis=0)
        g = g + dot_t(rows, w2t[ky])
    above = jnp.where(not_first, a1[8, :, 0:128] + s1[8, :, 0:128] * g[0:128], 0.0)
    below = jnp.where(not_last, a1[8, :, 128:256] + s1[8, :, 128:256] * g[128:256], 0.0)
    gp1[8] = jnp.concatenate([above, below], axis=1).astype(BF)

    g = jnp.zeros((128, 256), F32)
    for k in range(9):
        g = g + dot_t(gp1[k], wb[k])
    across = jnp.transpose(g)
    lined = jnp.concatenate([across[d * 64 : (d + 1) * 64] for d in range(4)], axis=1)
    back = jnp.concatenate([onehot(col == base + d - 1) for d in range(4)], axis=0)
    high = lined.astype(BF)
    low = (lined - high.astype(F32)).astype(BF)
    out = dot(high, back) + dot(low, back)
    grad_ref[0] = out[0:48].reshape(3, 16, 256)

    total = gathered_loss(cl, lall, DP)
    sums = jnp.sum(total, axis=1, keepdims=True)
    lanes = iota((8, 128), 1)
    counts = [32.0 * (128 >> s) * (256 >> s) for s in range(5)]
    scale = jnp.zeros((8, 128), F32)
    for s in range(5):
        scale = scale + jnp.where((lanes == s) & (rows_of == s), 1.0 / counts[s], 0.0)
    loss_ref[...] = jnp.sum(sums * scale, axis=0, keepdims=True)[:, 0:5]


def hand_on(losses_ref, grads_ref, loss_ref, grad_ref):
    loss_ref[...] = losses_ref[...]
    grad_ref[...] = grads_ref[...]


def on_device(*args):
    (real, fake, w1, w2, w3, w4, w5, *vectors) = args
    flat = [w.reshape(-1, w.shape[-1]) for w in (w2, w3, w4, w5)]
    vectors = [v.reshape(1, -1) for v in vectors]
    vmem = pl.BlockSpec(memory_space=pltpu.VMEM)
    anywhere = pl.BlockSpec(memory_space=pl.ANY)
    v = pltpu.VMEM
    dma = pltpu.SemaphoreType.DMA
    scratch = [
        v((3, 256, 128), BF), v((3, 128, 384), BF), v((1152, 256), BF), v((2304, 512), BF),
        v((4608, 512), BF), v((16, 512), F32), v((9, 256, 256), BF), v((8, 256), F32),
        v((5, 256, 256), BF),
        v((22, 256, 256), BF), v((10, 128, 384), BF), v((4, 64, 768), BF), v((10, 32, 1536), BF),
        v((12, 128, 384), BF), v((8, 64, 768), BF), v((6, 32, 1536), BF), v((12, 16, 1536), BF),
        v((9, 128, 256), BF),
        v((10, 256, 256), BF), v((10, 128, 256), F32), v((10, 512, 128), BF),
        v((10, 256, 128), F32), v((4, 256, 256), BF), v((4, 128, 256), F32),
        v((9, 128, 256), F32), v((9, 128, 256), F32), v((12, 128, 128), F32),
        v((12, 128, 128), F32), v((8, 64, 256), F32), v((8, 64, 256), F32),
        v((2, 32, 512), F32), v((2, 32, 512), F32),
        v((96, 256), BF), v((2, 96, 256), BF), v((32, 512), BF), v((8, 32, 512), BF),
        v((4, 32, 512), BF), v((2, 4, 32, 512), BF),
        v((5, 8, 128), F32), v((2, 8, 128), F32), v((8, 8, 128), F32), v((32, 8, 128), F32),
        dma((6,)), dma((2, 2)), dma((2, 2)), dma((7,)), dma((7,)), dma((40,)), dma((40,)),
    ]
    losses, grads = pl.pallas_call(
        body,
        out_shape=(
            jax.ShapeDtypeStruct((1, 5), F32),
            jax.ShapeDtypeStruct((1, 3, 16, 256), F32),
        ),
        in_specs=[vmem] * 3 + [anywhere] * 4 + [vmem] * 10,
        out_specs=(vmem, vmem),
        scratch_shapes=scratch,
        compiler_params=pltpu.CompilerParams(
            collective_id=0, has_side_effects=True, vmem_limit_bytes=56 << 20
        ),
        name="whole_step",
    )(real, fake, w1, *flat, *vectors)
    losses, grads = pl.pallas_call(
        hand_on,
        out_shape=(
            jax.ShapeDtypeStruct((1, 5), F32),
            jax.ShapeDtypeStruct((1, 3, 16, 256), F32),
        ),
        in_specs=[vmem] * 2,
        out_specs=(vmem, vmem),
        name="hand_on",
    )(losses, grads)
    return (losses.reshape(5), grads)


def solution(mesh):
    frames = P("dp", None, "rows", None)
    return jax.shard_map(
        on_device,
        mesh=mesh,
        in_specs=(frames, frames) + (P(),) * 15,
        out_specs=(P(), frames),
        check_vma=False,
    )
```

```python
import functools

import jax
import jax.numpy as jnp
from jax import lax
from jax.experimental import pallas as pl
from jax.experimental.pallas import tpu as pltpu
from jax.sharding import PartitionSpec as P

MESH = pl.DeviceIdType.MESH
F32 = jnp.float32
BF = jnp.bfloat16
EPS = 1e-06
ROOT = 0.7978845608028654
CUBE = 0.044715

ROWS = 8
NZ = 8
NY = 4


def dot(a, b):
    return lax.dot_general(a, b, (((1,), (0,)), ((), ())), preferred_element_type=F32)


def dot_t(a, b):
    return lax.dot_general(a, b, (((1,), (1,)), ((), ())), preferred_element_type=F32)


def iota(shape, dim):
    return lax.broadcasted_iota(jnp.int32, shape, dim)


def onehot(cond):
    return jnp.where(cond, 1.0, 0.0).astype(BF)


def rounded(x):
    return x.astype(BF).astype(F32)


def gelu(x):
    t = jnp.tanh(x * (ROOT + (ROOT * CUBE) * (x * x)))
    return x * (0.5 + 0.5 * t)


def gelu_both(x):
    x2 = x * x
    t = jnp.tanh(x * (ROOT + (ROOT * CUBE) * x2))
    h = 0.5 + 0.5 * t
    slope = h + (0.5 * x) * (1.0 - t * t) * (ROOT + (3.0 * ROOT * CUBE) * x2)
    return x * h, slope


def tap(r, f, lin, total):
    a = lax.rsqrt(total(r * r) + EPS)
    b = lax.rsqrt(total(f * f) + EPS)
    nf = f * b
    d = r * a - nf
    ld = lin * d
    grad = (ld - nf * total(nf * ld)) * (-2.0 * b)
    return ld * d, grad


def lane_sum(x):
    return jnp.sum(x, axis=-1, keepdims=True)


def fold(x):
    m, c = x.shape
    y = jnp.sum(x.reshape(m // 8, 8, c), axis=0)
    out = y[:, 0:128]
    for j in range(1, c // 128):
        out = out + y[:, j * 128 : (j + 1) * 128]
    return out


def shifted(v, phases):
    c = v.shape[-1]
    q = iota((16, c), 0)
    n = phases * 16
    tail = jnp.where(q < 15, pltpu.roll(v[0:16], 15, 0), 0.0)
    head = jnp.where(q > 0, pltpu.roll(v[n - 16 : n], 1, 0), 0.0)
    if phases == 1:
        return head, tail
    left = jnp.concatenate([head, v[0 : n - 16]], axis=0)
    right = jnp.concatenate([v[16:n], tail], axis=0)
    return left, right


def pool_cols(v, phases):
    c = v.shape[-1]
    return jnp.sum(v.reshape(phases // 2, 2, 16, c), axis=1).reshape(phases * 8, c)


def spread_cols(v, phases):
    c = v.shape[-1]
    y = jnp.broadcast_to(v.reshape(phases, 1, 16, c), (phases, 2, 16, c))
    return y.reshape(phases * 32, c)


def body(
    real_ref, fake_ref, w1_ref, w2_hbm, w3_hbm, w4_hbm, w5_hbm,
    b1_ref, b2_ref, b3_ref, b4_ref, b5_ref, l1_ref, l2_ref, l3_ref, l4_ref, l5_ref,
    loss_ref, grad_ref,
    w2s, w2t, w3s, w4s, w5s, wsm, wb, vec, tt,
    x2, x3, x4, x5, g2, g3, g4, g5, back,
    act1, sl1, act2, sl2, act3, sl3,
    a1, s1, a2, s2, a3, s3, a4, s4,
    stage0, land0, stage5, land5, stage4, land4,
    parts, own, lrow, lz, ly,
    wsem, ssem, rsem, gsend, grecv, lsend, lrecv,
):
    dp = lax.axis_index("dp")
    me = lax.axis_index("rows")
    zi = lax.rem(dp, NZ)
    yi = lax.div(dp, NZ)
    not_first = me > 0
    not_last = me < ROWS - 1

    def row_peer(k):
        return (dp, lax.rem(me + k, ROWS))

    def z_peer(k):
        return (yi * NZ + lax.rem(zi + k, NZ), me)

    def y_peer(k):
        return (lax.rem(yi + k, NY) * NZ + zi, me)

    cw2 = [
        pltpu.make_async_copy(
            w2_hbm.at[pl.ds(ky * 192, 192)],
            w2s.at[ky + half, pl.ds(0, 192), pl.ds(half * 128, 128)],
            wsem.at[2 * ky + half],
        )
        for ky in range(3)
        for half in range(2)
    ]
    cw3 = pltpu.make_async_copy(w3_hbm, w3s, wsem.at[6])
    cw4 = pltpu.make_async_copy(w4_hbm, w4s, wsem.at[7])
    cw5 = pltpu.make_async_copy(w5_hbm, w5s, wsem.at[8])
    for c in cw2 + [cw3, cw4, cw5]:
        c.start()

    barrier = pltpu.get_barrier_semaphore()
    peers = (
        [row_peer(k) for k in range(1, ROWS)]
        + [z_peer(k) for k in range(1, NZ)]
        + [y_peer(k) for k in range(1, NY)]
    )
    for peer in peers:
        pl.semaphore_signal(barrier, inc=1, device_id=peer, device_id_type=MESH)

    def beside(first, second, land, n):
        up = pltpu.make_async_remote_copy(
            src_ref=first, dst_ref=land.at[1], send_sem=ssem.at[n, 0],
            recv_sem=rsem.at[n, 1], device_id=row_peer(ROWS - 1), device_id_type=MESH,
        )
        down = pltpu.make_async_remote_copy(
            src_ref=second, dst_ref=land.at[0], send_sem=ssem.at[n, 1],
            recv_sem=rsem.at[n, 0], device_id=row_peer(1), device_id_type=MESH,
        )
        return up, down

    stage0[0:48] = real_ref[0].reshape(48, 256)
    stage0[48:96] = fake_ref[0].reshape(48, 256)

    wsm[...] = jnp.zeros_like(wsm)
    for ky in range(3):
        for kx in range(3):
            piece = w1_ref[ky, kx].astype(F32)
            for p in range(2):
                lane = (kx + p) * 128 + p * 64
                wsm[ky * 3 : ky * 3 + 3, lane : lane + 64] = piece
    small = wsm[...].astype(BF)

    for k in range(9):
        idx = iota((64, 16), 0)
        n = iota((64, 16), 1)
        ky = jnp.where(n >= 3, 1, 0) + jnp.where(n >= 6, 1, 0)
        ci = n - 3 * ky
        for half in range(2):
            row = 2 * k + half if k < 8 else 17 * half - 1
            at = row + ky - 1
            inner = (idx >> 4 == ci) & ((idx & 15) == at) & (idx < 48)
            above = (idx - 48 == ci) & (at == -1)
            below = (idx - 51 == ci) & (at == 16)
            block = dot(onehot((inner | above | below) & (n < 9)), small).astype(BF)
            for d in range(4):
                wb[k, d * 64 : (d + 1) * 64, half * 128 : (half + 1) * 128] = block[
                    :, d * 128 : (d + 1) * 128
                ]

    for row, ref in ((0, b1_ref), (1, l1_ref)):
        for q in range(4):
            vec[row : row + 1, q * 64 : (q + 1) * 64] = ref[...]
    for row, ref in ((2, b2_ref), (3, l2_ref)):
        for q in range(2):
            vec[row : row + 1, q * 128 : (q + 1) * 128] = ref[...]
    ones_part = onehot(iota((256, 256), 0) >> 6 == iota((256, 256), 1) >> 6)
    ones_rows = onehot(iota((256, 256), 0) >> 7 == iota((256, 256), 1) >> 7)

    def sum_part(x):
        return dot(x.astype(BF), ones_part)

    def sum_rows(x):
        return dot(x.astype(BF), ones_rows)

    parts[...] = jnp.zeros_like(parts)
    w2s[:, 192:256, :] = jnp.zeros((4, 64, 256), BF)
    w2s[0, 0:192, 128:256] = jnp.zeros((192, 128), BF)
    w2s[3, 0:192, 0:128] = jnp.zeros((192, 128), BF)

    pos = iota((128, 256), 0)
    col = iota((128, 256), 1)
    base = 16 * (pos & 15) + 2 * (pos >> 4)
    take = onehot(col == base)
    for d in range(4):
        back[d * 128 : (d + 1) * 128, :] = onehot(col == base + d - 1)

    def patches(slot, images, sources):
        for i in range(2):
            halo = jnp.zeros((16, 256), F32)
            for source, row, off, ok in sources:
                j = iota((16, 96), 0) - off
                k = iota((16, 96), 1)
                pick = (j >= 0) & (j < 3) & (k == i * 48 + j * 16 + row)
                if ok is not None:
                    pick = pick & ok
                halo = halo + dot(onehot(pick), source)
            whole = jnp.concatenate([images[i * 48 : (i + 1) * 48].astype(F32), halo], axis=0)
            cols = iota((64, 256), 1)
            turned = []
            for d in range(4):
                dx = d - 1
                moved = whole if dx == 0 else pltpu.roll(whole, (-dx) % 256, 1)
                moved = jnp.where((cols + dx >= 0) & (cols + dx < 256), moved, 0.0)
                turned.append(moved.astype(BF))
            tt[slot, i * 128 : (i + 1) * 128, :] = dot_t(
                take, jnp.concatenate(turned, axis=0)
            ).astype(BF)

    mine = stage0[...]
    patches(0, mine, ())

    pl.semaphore_wait(barrier, len(peers))
    c0 = beside(stage0, stage0, land0, 0)
    for c in c0:
        c.start()

    lane = iota((128, 128), 1)
    bias1 = vec[0:1, :]
    lin1 = vec[1:2, :]

    def put2(row, v):
        for i in range(2):
            w = v[i * 128 : (i + 1) * 128]
            left, right = shifted(w, 8)
            x2[row, i * 128 : (i + 1) * 128, 0:128] = jnp.where(lane < 64, left, w).astype(BF)
            x2[row, i * 128 : (i + 1) * 128, 128:256] = right.astype(BF)

    def segment1(slot, k, p, keep, ok):
        pre = dot(tt[slot], wb[k]) + bias1
        if keep is None:
            act = rounded(gelu(pre))
        else:
            act_f, slope = gelu_both(pre[128:256])
            act = rounded(jnp.concatenate([gelu(pre[0:128]), act_f], axis=0))
            if keep == "left":
                act1[8, :, 0:128] = act[:, 128:256].astype(BF)
                sl1[8, :, 0:128] = slope[:, 128:256]
            elif keep == "right":
                act1[8, :, 128:256] = act[:, 0:128].astype(BF)
                sl1[8, :, 128:256] = slope[:, 0:128]
            else:
                act1[k] = act.astype(BF)
                sl1[k] = slope
        s = act[:, 0:128] + act[:, 128:256]
        v = rounded((s + pltpu.roll(s, 64, 1)) * 0.25)
        if ok is not None:
            v = jnp.where(ok, v, 0.0)
        put2(p, v)

    def tap1(k, counted):
        act = act1[k].astype(F32)
        terms, grad = tap(act[0:128], act[128:256], lin1, sum_part)
        if counted:
            parts[0] += fold(terms)
        slope = sl1[k]
        a1[k] = slope * grad
        s1[k] = slope * 0.25

    for k in range(1, 7):
        segment1(0, k, 7 + k, "own", None)
    for k in range(1, 7):
        tap1(k, True)

    for c in cw2:
        c.wait()
    for at, ky in ((0, 0), (64, 2), (128, 1), (192, 1)):
        for kx in range(3):
            piece = w2s[ky, kx * 64 : (kx + 1) * 64, 0:128]
            w2t[at : at + 64, kx * 128 : (kx + 1) * 128] = piece

    def put(ref, row, v, phases, c):
        n = phases * 16
        for i in range(2):
            w = v[i * n : (i + 1) * n]
            left, right = shifted(w, phases)
            ref[row, i * n : (i + 1) * n, 0:c] = left.astype(BF)
            ref[row, i * n : (i + 1) * n, c : 2 * c] = w.astype(BF)
            ref[row, i * n : (i + 1) * n, 2 * c : 3 * c] = right.astype(BF)

    bias2 = vec[2:3, :]
    lin2 = vec[3:4, :]

    def segment2(m):
        pre = bias2
        for d in range(4):
            pre = pre + dot(x2[2 * m + d], w2s[d])
        if 2 <= m < 8:
            act_f, slope = gelu_both(pre[128:256])
            act = rounded(jnp.concatenate([gelu(pre[0:128]), act_f], axis=0))
            act2[m - 2] = act.astype(BF)
            sl2[m - 2] = slope
        else:
            act = rounded(gelu(pre))
        v = rounded(pool_cols(act[:, 0:128] + act[:, 128:256], 16) * 0.25)
        if m < 3:
            v = jnp.where(not_first, v, 0.0)
        if m >= 7:
            v = jnp.where(not_last, v, 0.0)
        put(x3, m, v, 4, 128)

    segment2(4)
    segment2(5)
    for c in c0:
        c.wait()
    upper = land0[0]
    lower = land0[1]
    patches(1, mine, ((upper, 15, 0, not_first), (lower, 0, 3, not_last)))
    patches(2, upper, ((mine, 0, 3, None),))
    patches(3, lower, ((mine, 15, 0, None),))
    segment1(2, 7, 6, "left", not_first)
    segment1(1, 0, 7, "own", None)
    segment1(1, 7, 14, "own", None)
    segment1(3, 0, 15, "right", not_last)

    for k in range(1, 7):
        segment1(2, k, k - 1, None, not_first)
        segment1(3, k, 15 + k, None, not_last)

    for m in (0, 1, 2, 3, 6, 7, 8, 9):
        segment2(m)

    def both(pre, n):
        parts_of = []
        slopes = []
        for row in range(2):
            top = 2 * row * n
            parts_of.append(gelu(pre[top : top + n]))
            act, slope = gelu_both(pre[top + n : top + 2 * n])
            parts_of.append(act)
            slopes.append(slope)
        return rounded(jnp.concatenate(parts_of, axis=0)), jnp.concatenate(slopes, axis=0)

    cw3.wait()

    def segment3(n):
        rows = [x3[2 * n + ky : 2 * n + ky + 2].reshape(256, 384) for ky in range(3)]
        pre = dot(jnp.concatenate(rows, axis=1), w3s[...]) + b3_ref[...]
        act, slope = both(pre, 64)
        act3[n] = act.astype(BF)
        sl3[n] = slope
        v = rounded(pool_cols(act[0:128] + act[128:256], 8) * 0.25)
        if n < 1:
            v = jnp.where(not_first, v, 0.0)
        if n >= 3:
            v = jnp.where(not_last, v, 0.0)
        put(x4, n, v, 2, 256)

    for n in range(4):
        segment3(n)

    cw4.wait()
    pre = b4_ref[...]
    for ky in range(3):
        rows = x4[ky : ky + 2].reshape(128, 768)
        pre = pre + dot(rows, w4s[ky * 768 : (ky + 1) * 768, :])
    act, slope = both(pre, 32)
    stage5[...] = (pool_cols(act[0:64] + act[64:128], 4) * 0.25).astype(BF)
    c5 = [
        pltpu.make_async_remote_copy(
            src_ref=stage5, dst_ref=land5.at[me], send_sem=gsend.at[k - 1],
            recv_sem=grecv.at[k - 1], device_id=row_peer(k), device_id_type=MESH,
        )
        for k in range(1, ROWS)
    ]
    for c in c5:
        c.start()
    land5[me] = stage5[...]

    act = act.reshape(2, 2, 32, 512)
    terms, grad = tap(
        act[:, 0].reshape(64, 512), act[:, 1].reshape(64, 512), l4_ref[...], lane_sum
    )
    parts[3] += fold(terms)
    a = slope * (64.0 * grad)
    s = slope * 0.25
    a4[...] = a.reshape(2, 32, 512)
    s4[...] = s.reshape(2, 32, 512)
    stage4[0:2] = a.astype(BF).reshape(2, 32, 512)
    stage4[2:4] = s.astype(BF).reshape(2, 32, 512)
    c4 = beside(stage4, stage4, land4, 1)
    for c in c4:
        c.start()

    def tap3(n, counted):
        act = act3[n].astype(F32).reshape(2, 2, 64, 256)
        slope = sl3[n]
        terms, grad = tap(
            act[:, 0].reshape(128, 256), act[:, 1].reshape(128, 256), l3_ref[...], lane_sum
        )
        if counted:
            parts[2] += fold(terms)
        a3[2 * n : 2 * n + 2] = (slope * (16.0 * grad)).reshape(2, 64, 256)
        s3[2 * n : 2 * n + 2] = (slope * 0.25).reshape(2, 64, 256)

    def tap2(m, counted):
        act = act2[m - 2].astype(F32)
        slope = sl2[m - 2]
        terms, grad = tap(act[0:128], act[128:256], lin2, sum_rows)
        if counted:
            parts[1] += fold(terms)
        a2[m - 2] = slope * (4.0 * grad)
        s2[m - 2] = slope * 0.25

    tap1(0, True)
    tap1(7, True)
    tap1(8, False)
    tap3(1, True)
    tap3(2, True)

    for m in range(3, 7):
        tap2(m, True)

    def spread_loss(src, land, slot, peer, count, first):
        copies = [
            pltpu.make_async_remote_copy(
                src_ref=src, dst_ref=land.at[slot], send_sem=lsend.at[first + k],
                recv_sem=lrecv.at[first + k], device_id=peer(k), device_id_type=MESH,
            )
            for k in range(1, count)
        ]
        for c in copies:
            c.start()
        land[slot] = src[...]
        return copies

    def gathered_loss(copies, land, count):
        for c in copies:
            c.wait()
        total = land[0]
        for j in range(1, count):
            total = total + land[j]
        return total

    rows_of = iota((8, 128), 0)
    sums = jnp.zeros((8, 128), F32)
    for s in range(4):
        sums = sums + jnp.where(rows_of == s, jnp.sum(parts[s], axis=0, keepdims=True), 0.0)
    own[0] = sums
    cl = spread_loss(own.at[0], lrow, me, row_peer, ROWS, 0)

    tap2(2, False)
    tap2(7, False)
    tap3(0, False)
    tap3(3, False)

    for row in (0, 9):
        x5[row] = jnp.zeros((32, 1536), BF)
    for row in (0, 1, 10, 11):
        g5[row] = jnp.zeros((16, 1536), BF)
    cw5.wait()
    for c in c5:
        c.wait()
    for row in range(ROWS):
        put(x5, row + 1, land5[row].astype(F32), 1, 512)
    pre = b5_ref[...]
    for ky in range(3):
        rows = x5[ky : ky + 8].reshape(256, 1536)
        pre = pre + dot(rows, w5s[ky * 1536 : (ky + 1) * 1536, :])
    pre = pre.reshape(8, 2, 16, 512)
    act_r = rounded(gelu(pre[:, 0].reshape(128, 512)))
    act_f, slope = gelu_both(pre[:, 1].reshape(128, 512))
    act_f = rounded(act_f)
    terms, grad = tap(act_r, act_f, l5_ref[...], lane_sum)
    gpre = rounded(slope * (256.0 * grad))

    def put_back(ref, row, v, phases, c):
        left, right = shifted(v, phases)
        ref[row, :, 0:c] = right.astype(BF)
        ref[row, :, c : 2 * c] = v.astype(BF)
        ref[row, :, 2 * c : 3 * c] = left.astype(BF)

    for row in range(ROWS):
        put_back(g5, row + 2, gpre[row * 16 : (row + 1) * 16], 1, 512)
    fifth = jnp.sum(fold(terms), axis=0, keepdims=True)
    own[1] = gathered_loss(cl, lrow, ROWS) + jnp.where(rows_of == 4, fifth, 0.0)
    cl = spread_loss(own.at[1], lz, zi, z_peer, NZ, 8)

    gin = jnp.zeros((48, 512), F32)
    for ky in range(3):
        rows = g5[pl.ds(me + 2 - ky, 3)].reshape(48, 1536)
        for kx in range(3):
            n = (ky * 3 + kx) * 512
            gin = gin + dot_t(rows[:, kx * 512 : (kx + 1) * 512], w5s[n : n + 512, :])

    for c in c4:
        c.wait()
    for u in range(6):
        wide = spread_cols(gin[(u // 2) * 16 : (u // 2 + 1) * 16], 1)
        if 2 <= u < 4:
            v = a4[u - 2] + s4[u - 2] * wide
        else:
            side, j, ok = (0, u, not_first) if u < 2 else (1, u - 4, not_last)
            a = land4[side, j].astype(F32)
            s = land4[side, 2 + j].astype(F32)
            v = jnp.where(ok, a + s * wide, 0.0)
        put_back(g4, u, rounded(v), 2, 512)
    gin = jnp.zeros((128, 256), F32)
    for ky in range(3):
        rows = g4[2 - ky : 6 - ky].reshape(128, 1536)
        for kx in range(3):
            n = (ky * 3 + kx) * 256
            gin = gin + dot_t(rows[:, kx * 512 : (kx + 1) * 512], w4s[n : n + 256, :])

    for j in range(8):
        wide = spread_cols(gin[(j // 2) * 32 : (j // 2 + 1) * 32], 2)
        v = a3[j] + s3[j] * wide
        if j < 2:
            v = jnp.where(not_first, v, 0.0)
        if j >= 6:
            v = jnp.where(not_last, v, 0.0)
        put_back(g3, j, rounded(v), 4, 256)
    gin = 0.0
    for ky in range(3):
        rows = g3[2 - ky : 8 - ky].reshape(384, 768)
        for kx in range(3):
            n = (ky * 3 + kx) * 128
            gin = gin + dot_t(rows[:, kx * 256 : (kx + 1) * 256], w3s[n : n + 128, :])
    own[2] = gathered_loss(cl, lz, NZ)
    cl = spread_loss(own.at[2], ly, yi, y_peer, NY, 16)

    for j in range(12):
        wide = spread_cols(gin[(j // 2) * 64 : (j // 2 + 1) * 64], 4)
        at = (j % 2) * 128
        v = a2[j // 2, :, at : at + 128] + s2[j // 2, :, at : at + 128] * wide
        if j < 2:
            v = jnp.where(not_first, v, 0.0)
        if j >= 10:
            v = jnp.where(not_last, v, 0.0)
        put_back(g2, j, rounded(v), 8, 128)

    products = []
    for n in range(6):
        two = dot_t(g2[2 * n : 2 * n + 2].reshape(256, 384), w2t[...])
        products += [two[0:128], two[128:256]]

    def gin2(z):
        u = jnp.where(lane < 64, products[z + 2][:, 0:128], products[z][:, 0:128])
        return u + pltpu.roll(u, 64, 1) + products[z + 1][:, 128:256]

    across = jnp.zeros((256, 128), F32)
    for k in range(9):
        if k < 8:
            g = gin2(k + 1)
            wide = jnp.concatenate([g, g], axis=1)
            v = a1[k] + s1[k] * wide
        else:
            above = a1[8, :, 0:128] + s1[8, :, 0:128] * gin2(0)
            below = a1[8, :, 128:256] + s1[8, :, 128:256] * gin2(9)
            v = jnp.concatenate(
                [jnp.where(not_first, above, 0.0), jnp.where(not_last, below, 0.0)], axis=1
            )
        across = across + dot_t(wb[k], v.astype(BF))
    lined = jnp.concatenate([across[d * 64 : (d + 1) * 64] for d in range(4)], axis=1)
    high = lined.astype(BF)
    low = (lined - high.astype(F32)).astype(BF)
    out = dot(high, back[...]) + dot(low, back[...])
    grad_ref[0] = out[0:48].reshape(3, 16, 256)

    total = gathered_loss(cl, ly, NY)
    sums = jnp.sum(total, axis=1, keepdims=True)
    lanes = iota((8, 128), 1)
    counts = [32.0 * (128 >> s) * (256 >> s) for s in range(5)]
    scale = jnp.zeros((8, 128), F32)
    for s in range(5):
        scale = scale + jnp.where((lanes == s) & (rows_of == s), 1.0 / counts[s], 0.0)
    loss_ref[...] = jnp.sum(sums * scale, axis=0, keepdims=True)[:, 0:5]


def hand_on(losses_ref, grads_ref, loss_ref, grad_ref):
    loss_ref[...] = losses_ref[...]
    grad_ref[...] = grads_ref[...]


def on_device(*args):
    (real, fake, w1, w2, w3, w4, w5, *vectors) = args
    flat = [w.reshape(-1, w.shape[-1]) for w in (w2, w3, w4, w5)]
    vectors = [v.reshape(1, -1) for v in vectors]
    vmem = pl.BlockSpec(memory_space=pltpu.VMEM)
    anywhere = pl.BlockSpec(memory_space=pl.ANY)
    v = pltpu.VMEM
    dma = pltpu.SemaphoreType.DMA
    scratch = [
        v((4, 256, 256), BF), v((256, 384), BF), v((1152, 256), BF), v((2304, 512), BF),
        v((4608, 512), BF), v((16, 512), F32), v((9, 256, 256), BF), v((8, 256), F32),
        v((4, 256, 256), BF),
        v((22, 256, 256), BF), v((10, 128, 384), BF), v((4, 64, 768), BF), v((10, 32, 1536), BF),
        v((12, 128, 384), BF), v((8, 64, 768), BF), v((6, 32, 1536), BF), v((12, 16, 1536), BF),
        v((512, 256), BF),
        v((9, 256, 256), BF), v((9, 128, 256), F32), v((6, 256, 256), BF),
        v((6, 128, 256), F32), v((4, 256, 256), BF), v((4, 128, 256), F32),
        v((9, 128, 256), F32), v((9, 128, 256), F32), v((6, 128, 256), F32),
        v((6, 128, 256), F32), v((8, 64, 256), F32), v((8, 64, 256), F32),
        v((2, 32, 512), F32), v((2, 32, 512), F32),
        v((96, 256), BF), v((2, 96, 256), BF), v((32, 512), BF), v((8, 32, 512), BF),
        v((4, 32, 512), BF), v((2, 4, 32, 512), BF),
        v((5, 8, 128), F32), v((3, 8, 128), F32), v((8, 8, 128), F32), v((8, 8, 128), F32),
        v((4, 8, 128), F32),
        dma((9,)), dma((2, 2)), dma((2, 2)), dma((7,)), dma((7,)), dma((24,)), dma((24,)),
    ]
    losses, grads = pl.pallas_call(
        body,
        out_shape=(
            jax.ShapeDtypeStruct((1, 5), F32),
            jax.ShapeDtypeStruct((1, 3, 16, 256), F32),
        ),
        in_specs=[vmem] * 3 + [anywhere] * 4 + [vmem] * 10,
        out_specs=(vmem, vmem),
        scratch_shapes=scratch,
        compiler_params=pltpu.CompilerParams(
            collective_id=0, has_side_effects=True, vmem_limit_bytes=56 << 20
        ),
        name="whole_step",
    )(real, fake, w1, *flat, *vectors)
    losses, grads = pl.pallas_call(
        hand_on,
        out_shape=(
            jax.ShapeDtypeStruct((1, 5), F32),
            jax.ShapeDtypeStruct((1, 3, 16, 256), F32),
        ),
        in_specs=[vmem] * 2,
        out_specs=(vmem, vmem),
        name="hand_on",
    )(losses, grads)
    return (losses.reshape(5), grads)


def solution(mesh):
    frames = P("dp", None, "rows", None)
    return jax.shard_map(
        on_device,
        mesh=mesh,
        in_specs=(frames, frames) + (P(),) * 15,
        out_specs=(P(), frames),
        check_vma=False,
    )
```

```python
import functools

import jax
import jax.numpy as jnp
from jax import lax
from jax.experimental import pallas as pl
from jax.experimental.pallas import tpu as pltpu
from jax.sharding import PartitionSpec as P

MESH = pl.DeviceIdType.MESH
F32 = jnp.float32
BF = jnp.bfloat16
EPS = 1e-06
ROOT = 0.7978845608028654
CUBE = 0.044715

ROWS = 8
NZ = 8
NY = 4


def dot(a, b):
    return lax.dot_general(a, b, (((1,), (0,)), ((), ())), preferred_element_type=F32)


def dot_t(a, b):
    return lax.dot_general(a, b, (((1,), (1,)), ((), ())), preferred_element_type=F32)


def iota(shape, dim):
    return lax.broadcasted_iota(jnp.int32, shape, dim)


def onehot(cond):
    return jnp.where(cond, 1.0, 0.0).astype(BF)


def rounded(x):
    return x.astype(BF).astype(F32)


def gelu(h):
    t = jnp.tanh(h * (2.0 * ROOT + (8.0 * ROOT * CUBE) * (h * h)))
    return h + h * t


def gelu_both(h):
    h2 = h * h
    t = jnp.tanh(h * (2.0 * ROOT + (8.0 * ROOT * CUBE) * h2))
    ht = h * t
    slope = (0.5 + 0.5 * t) + (h - ht * t) * (ROOT + (12.0 * ROOT * CUBE) * h2)
    return h + ht, slope


def tap(r, f, lin, total):
    a = lax.rsqrt(total(r * r) + EPS)
    b = lax.rsqrt(total(f * f) + EPS)
    nf = f * b
    d = r * a - nf
    ld = lin * d
    grad = (ld - nf * total(nf * ld)) * (-2.0 * b)
    return ld * d, grad


def lane_sum(x):
    return jnp.sum(x, axis=-1, keepdims=True)


def fold(x):
    m, c = x.shape
    y = jnp.sum(x.reshape(m // 8, 8, c), axis=0)
    out = y[:, 0:128]
    for j in range(1, c // 128):
        out = out + y[:, j * 128 : (j + 1) * 128]
    return out


def shifted(v, phases):
    c = v.shape[-1]
    q = iota((16, c), 0)
    n = phases * 16
    tail = jnp.where(q < 15, pltpu.roll(v[0:16], 15, 0), 0.0)
    head = jnp.where(q > 0, pltpu.roll(v[n - 16 : n], 1, 0), 0.0)
    if phases == 1:
        return head, tail
    left = jnp.concatenate([head, v[0 : n - 16]], axis=0)
    right = jnp.concatenate([v[16:n], tail], axis=0)
    return left, right


def pool_cols(v, phases):
    c = v.shape[-1]
    return jnp.sum(v.reshape(phases // 2, 2, 16, c), axis=1).reshape(phases * 8, c)


def spread_cols(v, phases):
    c = v.shape[-1]
    y = jnp.broadcast_to(v.reshape(phases, 1, 16, c), (phases, 2, 16, c))
    return y.reshape(phases * 32, c)


def body(
    real_hbm, fake_hbm, w1_hbm, w2_hbm, w3_hbm, w4_hbm, w5_hbm,
    b1_hbm, b2_hbm, b3_hbm, b4_hbm, b5_hbm, l1_hbm, l2_hbm, l3_hbm, l4_hbm, l5_hbm,
    loss_ref, grad_ref,
    real_ref, fake_ref, w1_ref,
    b1_ref, b2_ref, b3_ref, b4_ref, b5_ref, l1_ref, l2_ref, l3_ref, l4_ref, l5_ref,
    w2s, w2t, w3s, w4s, w5s, wsm, wb, vec, tt,
    x2, x3, x4, x5, g2, g3, g4, g5, back,
    act1, sl1, act2, sl2, act3, sl3,
    a1, s1, a2, s2, a3, s3, a4, s4,
    stage0, land0, stage5, land5, stage4, land4,
    parts, own, lrow, lz, ly,
    isem, wsem, ssem, rsem, gsend, grecv, lsend, lrecv,
):
    dp = lax.axis_index("dp")
    me = lax.axis_index("rows")
    zi = lax.rem(dp, NZ)
    yi = lax.div(dp, NZ)
    not_first = me > 0
    not_last = me < ROWS - 1

    def row_peer(k):
        return (dp, lax.rem(me + k, ROWS))

    def z_peer(k):
        return (yi * NZ + lax.rem(zi + k, NZ), me)

    def y_peer(k):
        return (lax.rem(yi + k, NY) * NZ + zi, me)

    barrier = pltpu.get_barrier_semaphore()
    peers = (
        [row_peer(k) for k in range(1, ROWS)]
        + [z_peer(k) for k in range(1, NZ)]
        + [y_peer(k) for k in range(1, NY)]
    )
    for peer in peers:
        pl.semaphore_signal(barrier, inc=1, device_id=peer, device_id_type=MESH)

    small_inputs = (
        (real_hbm, real_ref), (fake_hbm, fake_ref), (w1_hbm, w1_ref),
        (b1_hbm, b1_ref), (b2_hbm, b2_ref), (b3_hbm, b3_ref), (b4_hbm, b4_ref), (b5_hbm, b5_ref),
        (l1_hbm, l1_ref), (l2_hbm, l2_ref), (l3_hbm, l3_ref), (l4_hbm, l4_ref), (l5_hbm, l5_ref),
    )
    ci = [
        pltpu.make_async_copy(src, dst, isem.at[n]) for n, (src, dst) in enumerate(small_inputs)
    ]
    for c in ci:
        c.start()

    cw2 = [
        pltpu.make_async_copy(
            w2_hbm.at[pl.ds(ky * 192, 192)],
            w2s.at[ky + half, pl.ds(0, 192), pl.ds(half * 128, 128)],
            wsem.at[2 * ky + half],
        )
        for ky in range(3)
        for half in range(2)
    ]
    cw3 = pltpu.make_async_copy(w3_hbm, w3s, wsem.at[6])
    cw4 = pltpu.make_async_copy(w4_hbm, w4s, wsem.at[7])
    cw5 = pltpu.make_async_copy(w5_hbm, w5s, wsem.at[8])
    for c in cw2 + [cw3, cw4, cw5]:
        c.start()


    def beside(first, second, land, n):
        up = pltpu.make_async_remote_copy(
            src_ref=first, dst_ref=land.at[1], send_sem=ssem.at[n, 0],
            recv_sem=rsem.at[n, 1], device_id=row_peer(ROWS - 1), device_id_type=MESH,
        )
        down = pltpu.make_async_remote_copy(
            src_ref=second, dst_ref=land.at[0], send_sem=ssem.at[n, 1],
            recv_sem=rsem.at[n, 0], device_id=row_peer(1), device_id_type=MESH,
        )
        return up, down

    for c in ci:
        c.wait()
    stage0[0:48] = real_ref[0].reshape(48, 256)
    stage0[48:96] = fake_ref[0].reshape(48, 256)

    wsm[...] = jnp.zeros_like(wsm)
    for ky in range(3):
        for kx in range(3):
            piece = w1_ref[ky, kx].astype(F32) * 0.5
            for p in range(2):
                lane = (kx + p) * 128 + p * 64
                wsm[ky * 3 : ky * 3 + 3, lane : lane + 64] = piece
    small = wsm[...].astype(BF)

    for k in range(9):
        idx = iota((64, 16), 0)
        n = iota((64, 16), 1)
        ky = jnp.where(n >= 3, 1, 0) + jnp.where(n >= 6, 1, 0)
        ci = n - 3 * ky
        for half in range(2):
            row = 2 * k + half if k < 8 else 17 * half - 1
            at = row + ky - 1
            inner = (idx >> 4 == ci) & ((idx & 15) == at) & (idx < 48)
            above = (idx - 48 == ci) & (at == -1)
            below = (idx - 51 == ci) & (at == 16)
            block = dot(onehot((inner | above | below) & (n < 9)), small).astype(BF)
            for d in range(4):
                wb[k, d * 64 : (d + 1) * 64, half * 128 : (half + 1) * 128] = block[
                    :, d * 128 : (d + 1) * 128
                ]

    for row, ref, scale in ((0, b1_ref, 0.5), (1, l1_ref, 1.0)):
        for q in range(4):
            vec[row : row + 1, q * 64 : (q + 1) * 64] = ref[...] * scale
    for row, ref, scale in ((2, b2_ref, 0.5), (3, l2_ref, 1.0)):
        for q in range(2):
            vec[row : row + 1, q * 128 : (q + 1) * 128] = ref[...] * scale
    ones_part = onehot(iota((256, 256), 0) >> 6 == iota((256, 256), 1) >> 6)
    ones_rows = onehot(iota((256, 256), 0) >> 7 == iota((256, 256), 1) >> 7)

    def sum_part(x):
        return dot(x.astype(BF), ones_part)

    def sum_rows(x):
        return dot(x.astype(BF), ones_rows)

    parts[...] = jnp.zeros_like(parts)
    w2s[:, 192:256, :] = jnp.zeros((4, 64, 256), BF)
    w2s[0, 0:192, 128:256] = jnp.zeros((192, 128), BF)
    w2s[3, 0:192, 0:128] = jnp.zeros((192, 128), BF)

    pos = iota((128, 256), 0)
    col = iota((128, 256), 1)
    base = 16 * (pos & 15) + 2 * (pos >> 4)
    take = onehot(col == base)
    for d in range(4):
        back[d * 128 : (d + 1) * 128, :] = onehot(col == base + d - 1)

    def patches(slot, images, sources):
        for i in range(2):
            halo = jnp.zeros((16, 256), F32)
            for source, row, off, ok in sources:
                j = iota((16, 96), 0) - off
                k = iota((16, 96), 1)
                pick = (j >= 0) & (j < 3) & (k == i * 48 + j * 16 + row)
                if ok is not None:
                    pick = pick & ok
                halo = halo + dot(onehot(pick), source)
            whole = jnp.concatenate([images[i * 48 : (i + 1) * 48].astype(F32), halo], axis=0)
            cols = iota((64, 256), 1)
            turned = []
            for d in range(4):
                dx = d - 1
                moved = whole if dx == 0 else pltpu.roll(whole, (-dx) % 256, 1)
                moved = jnp.where((cols + dx >= 0) & (cols + dx < 256), moved, 0.0)
                turned.append(moved.astype(BF))
            tt[slot, i * 128 : (i + 1) * 128, :] = dot_t(
                take, jnp.concatenate(turned, axis=0)
            ).astype(BF)

    mine = stage0[...]
    patches(0, mine, ())

    pl.semaphore_wait(barrier, len(peers))
    c0 = beside(stage0, stage0, land0, 0)
    for c in c0:
        c.start()

    lane = iota((128, 128), 1)
    bias1 = vec[0:1, :]
    lin1 = vec[1:2, :]

    def put2(row, v):
        for i in range(2):
            w = v[i * 128 : (i + 1) * 128]
            left, right = shifted(w, 8)
            x2[row, i * 128 : (i + 1) * 128, 0:128] = jnp.where(lane < 64, left, w).astype(BF)
            x2[row, i * 128 : (i + 1) * 128, 128:256] = right.astype(BF)

    def segment1(slot, k, p, keep, ok):
        pre = dot(tt[slot], wb[k]) + bias1
        if keep is None:
            act = rounded(gelu(pre))
        else:
            act_f, slope = gelu_both(pre[128:256])
            act = rounded(jnp.concatenate([gelu(pre[0:128]), act_f], axis=0))
            if keep == "left":
                act1[8, :, 0:128] = act[:, 128:256].astype(BF)
                sl1[8, :, 0:128] = slope[:, 128:256]
            elif keep == "right":
                act1[8, :, 128:256] = act[:, 0:128].astype(BF)
                sl1[8, :, 128:256] = slope[:, 0:128]
            else:
                act1[k] = act.astype(BF)
                sl1[k] = slope
        s = act[:, 0:128] + act[:, 128:256]
        v = rounded((s + pltpu.roll(s, 64, 1)) * 0.125)
        if ok is not None:
            v = jnp.where(ok, v, 0.0)
        put2(p, v)

    def tap1(k, counted):
        act = act1[k].astype(F32)
        terms, grad = tap(act[0:128], act[128:256], lin1, sum_part)
        if counted:
            parts[0] += fold(terms)
        slope = sl1[k]
        a1[k] = slope * grad
        s1[k] = slope * 0.25

    for k in range(1, 7):
        segment1(0, k, 7 + k, "own", None)
    for k in range(1, 7):
        tap1(k, True)

    for c in cw2:
        c.wait()
    for at, ky in ((0, 0), (64, 2), (128, 1), (192, 1)):
        for kx in range(3):
            piece = w2s[ky, kx * 64 : (kx + 1) * 64, 0:128]
            w2t[at : at + 64, kx * 128 : (kx + 1) * 128] = piece

    def put(ref, row, v, phases, c):
        n = phases * 16
        for i in range(2):
            w = v[i * n : (i + 1) * n]
            left, right = shifted(w, phases)
            ref[row, i * n : (i + 1) * n, 0:c] = left.astype(BF)
            ref[row, i * n : (i + 1) * n, c : 2 * c] = w.astype(BF)
            ref[row, i * n : (i + 1) * n, 2 * c : 3 * c] = right.astype(BF)

    bias2 = vec[2:3, :]
    lin2 = vec[3:4, :]

    def segment2(m):
        pre = bias2
        for d in range(4):
            pre = pre + dot(x2[2 * m + d], w2s[d])
        if 2 <= m < 8:
            act_f, slope = gelu_both(pre[128:256])
            act = rounded(jnp.concatenate([gelu(pre[0:128]), act_f], axis=0))
            act2[m - 2] = act.astype(BF)
            sl2[m - 2] = slope
        else:
            act = rounded(gelu(pre))
        v = rounded(pool_cols(act[:, 0:128] + act[:, 128:256], 16) * 0.125)
        if m < 3:
            v = jnp.where(not_first, v, 0.0)
        if m >= 7:
            v = jnp.where(not_last, v, 0.0)
        put(x3, m, v, 4, 128)

    segment2(4)
    segment2(5)
    for c in c0:
        c.wait()
    upper = land0[0]
    lower = land0[1]
    patches(1, mine, ((upper, 15, 0, not_first), (lower, 0, 3, not_last)))
    patches(2, upper, ((mine, 0, 3, None),))
    patches(3, lower, ((mine, 15, 0, None),))
    segment1(2, 7, 6, "left", not_first)
    segment1(1, 0, 7, "own", None)
    segment1(1, 7, 14, "own", None)
    segment1(3, 0, 15, "right", not_last)

    for k in range(1, 7):
        segment1(2, k, k - 1, None, not_first)
        segment1(3, k, 15 + k, None, not_last)

    for m in (0, 1, 2, 3, 6, 7, 8, 9):
        segment2(m)

    def both(pre, n):
        parts_of = []
        slopes = []
        for row in range(2):
            top = 2 * row * n
            parts_of.append(gelu(pre[top : top + n]))
            act, slope = gelu_both(pre[top + n : top + 2 * n])
            parts_of.append(act)
            slopes.append(slope)
        return rounded(jnp.concatenate(parts_of, axis=0)), jnp.concatenate(slopes, axis=0)

    cw3.wait()

    def segment3(n):
        rows = [x3[2 * n + ky : 2 * n + ky + 2].reshape(256, 384) for ky in range(3)]
        pre = dot(jnp.concatenate(rows, axis=1), w3s[...]) + b3_ref[...] * 0.5
        act, slope = both(pre, 64)
        act3[n] = act.astype(BF)
        sl3[n] = slope
        v = rounded(pool_cols(act[0:128] + act[128:256], 8) * 0.125)
        if n < 1:
            v = jnp.where(not_first, v, 0.0)
        if n >= 3:
            v = jnp.where(not_last, v, 0.0)
        put(x4, n, v, 2, 256)

    for n in range(4):
        segment3(n)

    cw4.wait()
    pre = b4_ref[...] * 0.5
    for ky in range(3):
        rows = x4[ky : ky + 2].reshape(128, 768)
        pre = pre + dot(rows, w4s[ky * 768 : (ky + 1) * 768, :])
    act, slope = both(pre, 32)
    stage5[...] = (pool_cols(act[0:64] + act[64:128], 4) * 0.125).astype(BF)
    c5 = [
        pltpu.make_async_remote_copy(
            src_ref=stage5, dst_ref=land5.at[me], send_sem=gsend.at[k - 1],
            recv_sem=grecv.at[k - 1], device_id=row_peer(k), device_id_type=MESH,
        )
        for k in range(1, ROWS)
    ]
    for c in c5:
        c.start()
    land5[me] = stage5[...]

    act = act.reshape(2, 2, 32, 512)
    terms, grad = tap(
        act[:, 0].reshape(64, 512), act[:, 1].reshape(64, 512), l4_ref[...], lane_sum
    )
    parts[3] += fold(terms)
    a = slope * (64.0 * grad)
    s = slope * 0.25
    a4[...] = a.reshape(2, 32, 512)
    s4[...] = s.reshape(2, 32, 512)
    stage4[0:2] = a.astype(BF).reshape(2, 32, 512)
    stage4[2:4] = s.astype(BF).reshape(2, 32, 512)
    c4 = beside(stage4, stage4, land4, 1)
    for c in c4:
        c.start()

    def tap3(n, counted):
        act = act3[n].astype(F32).reshape(2, 2, 64, 256)
        slope = sl3[n]
        terms, grad = tap(
            act[:, 0].reshape(128, 256), act[:, 1].reshape(128, 256), l3_ref[...], lane_sum
        )
        if counted:
            parts[2] += fold(terms)
        a3[2 * n : 2 * n + 2] = (slope * (16.0 * grad)).reshape(2, 64, 256)
        s3[2 * n : 2 * n + 2] = (slope * 0.25).reshape(2, 64, 256)

    def tap2(m, counted):
        act = act2[m - 2].astype(F32)
        slope = sl2[m - 2]
        terms, grad = tap(act[0:128], act[128:256], lin2, sum_rows)
        if counted:
            parts[1] += fold(terms)
        a2[m - 2] = slope * (4.0 * grad)
        s2[m - 2] = slope * 0.25

    tap1(0, True)
    tap1(7, True)
    tap1(8, False)
    tap3(1, True)
    tap3(2, True)

    for m in range(3, 7):
        tap2(m, True)

    def spread_loss(src, land, slot, peer, count, first):
        copies = [
            pltpu.make_async_remote_copy(
                src_ref=src, dst_ref=land.at[slot], send_sem=lsend.at[first + k],
                recv_sem=lrecv.at[first + k], device_id=peer(k), device_id_type=MESH,
            )
            for k in range(1, count)
        ]
        for c in copies:
            c.start()
        land[slot] = src[...]
        return copies

    def gathered_loss(copies, land, count):
        for c in copies:
            c.wait()
        total = land[0]
        for j in range(1, count):
            total = total + land[j]
        return total

    rows_of = iota((8, 128), 0)
    sums = jnp.zeros((8, 128), F32)
    for s in range(4):
        sums = sums + jnp.where(rows_of == s, jnp.sum(parts[s], axis=0, keepdims=True), 0.0)
    own[0] = sums
    cl = spread_loss(own.at[0], lrow, me, row_peer, ROWS, 0)

    tap2(2, False)
    tap2(7, False)
    tap3(0, False)
    tap3(3, False)

    for row in (0, 9):
        x5[row] = jnp.zeros((32, 1536), BF)
    for row in (0, 1, 10, 11):
        g5[row] = jnp.zeros((16, 1536), BF)
    cw5.wait()
    for c in c5:
        c.wait()
    for row in range(ROWS):
        put(x5, row + 1, land5[row].astype(F32), 1, 512)
    pre = b5_ref[...] * 0.5
    for ky in range(3):
        rows = x5[ky : ky + 8].reshape(256, 1536)
        pre = pre + dot(rows, w5s[ky * 1536 : (ky + 1) * 1536, :])
    pre = pre.reshape(8, 2, 16, 512)
    act_r = rounded(gelu(pre[:, 0].reshape(128, 512)))
    act_f, slope = gelu_both(pre[:, 1].reshape(128, 512))
    act_f = rounded(act_f)
    terms, grad = tap(act_r, act_f, l5_ref[...], lane_sum)
    gpre = rounded(slope * (256.0 * grad))

    def put_back(ref, row, v, phases, c):
        left, right = shifted(v, phases)
        ref[row, :, 0:c] = right.astype(BF)
        ref[row, :, c : 2 * c] = v.astype(BF)
        ref[row, :, 2 * c : 3 * c] = left.astype(BF)

    for row in range(ROWS):
        put_back(g5, row + 2, gpre[row * 16 : (row + 1) * 16], 1, 512)
    fifth = jnp.sum(fold(terms), axis=0, keepdims=True)
    own[1] = gathered_loss(cl, lrow, ROWS) + jnp.where(rows_of == 4, fifth, 0.0)
    cl = spread_loss(own.at[1], lz, zi, z_peer, NZ, 8)

    gin = jnp.zeros((48, 512), F32)
    for ky in range(3):
        rows = g5[pl.ds(me + 2 - ky, 3)].reshape(48, 1536)
        for kx in range(3):
            n = (ky * 3 + kx) * 512
            gin = gin + dot_t(rows[:, kx * 512 : (kx + 1) * 512], w5s[n : n + 512, :])

    for c in c4:
        c.wait()
    for u in range(6):
        wide = spread_cols(gin[(u // 2) * 16 : (u // 2 + 1) * 16], 1)
        if 2 <= u < 4:
            v = a4[u - 2] + s4[u - 2] * wide
        else:
            side, j, ok = (0, u, not_first) if u < 2 else (1, u - 4, not_last)
            a = land4[side, j].astype(F32)
            s = land4[side, 2 + j].astype(F32)
            v = jnp.where(ok, a + s * wide, 0.0)
        put_back(g4, u, rounded(v), 2, 512)
    gin = jnp.zeros((128, 256), F32)
    for ky in range(3):
        rows = g4[2 - ky : 6 - ky].reshape(128, 1536)
        for kx in range(3):
            n = (ky * 3 + kx) * 256
            gin = gin + dot_t(rows[:, kx * 512 : (kx + 1) * 512], w4s[n : n + 256, :])

    for j in range(8):
        wide = spread_cols(gin[(j // 2) * 32 : (j // 2 + 1) * 32], 2)
        v = a3[j] + s3[j] * wide
        if j < 2:
            v = jnp.where(not_first, v, 0.0)
        if j >= 6:
            v = jnp.where(not_last, v, 0.0)
        put_back(g3, j, rounded(v), 4, 256)
    gin = 0.0
    for ky in range(3):
        rows = g3[2 - ky : 8 - ky].reshape(384, 768)
        for kx in range(3):
            n = (ky * 3 + kx) * 128
            gin = gin + dot_t(rows[:, kx * 256 : (kx + 1) * 256], w3s[n : n + 128, :])
    own[2] = gathered_loss(cl, lz, NZ)
    cl = spread_loss(own.at[2], ly, yi, y_peer, NY, 16)

    for j in range(12):
        wide = spread_cols(gin[(j // 2) * 64 : (j // 2 + 1) * 64], 4)
        at = (j % 2) * 128
        v = a2[j // 2, :, at : at + 128] + s2[j // 2, :, at : at + 128] * wide
        if j < 2:
            v = jnp.where(not_first, v, 0.0)
        if j >= 10:
            v = jnp.where(not_last, v, 0.0)
        put_back(g2, j, rounded(v), 8, 128)

    products = []
    for n in range(6):
        two = dot_t(g2[2 * n : 2 * n + 2].reshape(256, 384), w2t[...])
        products += [two[0:128], two[128:256]]

    def gin2(z):
        u = jnp.where(lane < 64, products[z + 2][:, 0:128], products[z][:, 0:128])
        return u + pltpu.roll(u, 64, 1) + products[z + 1][:, 128:256]

    across = jnp.zeros((256, 128), F32)
    for k in range(9):
        if k < 8:
            g = gin2(k + 1)
            wide = jnp.concatenate([g, g], axis=1)
            v = a1[k] + s1[k] * wide
        else:
            above = a1[8, :, 0:128] + s1[8, :, 0:128] * gin2(0)
            below = a1[8, :, 128:256] + s1[8, :, 128:256] * gin2(9)
            v = jnp.concatenate(
                [jnp.where(not_first, above, 0.0), jnp.where(not_last, below, 0.0)], axis=1
            )
        across = across + dot_t(wb[k], v.astype(BF))
    across = across * 2.0
    lined = jnp.concatenate([across[d * 64 : (d + 1) * 64] for d in range(4)], axis=1)
    high = lined.astype(BF)
    low = (lined - high.astype(F32)).astype(BF)
    out = dot(high, back[...]) + dot(low, back[...])
    grad_ref[0] = out[0:48].reshape(3, 16, 256)

    total = gathered_loss(cl, ly, NY)
    sums = jnp.sum(total, axis=1, keepdims=True)
    lanes = iota((8, 128), 1)
    counts = [32.0 * (128 >> s) * (256 >> s) for s in range(5)]
    scale = jnp.zeros((8, 128), F32)
    for s in range(5):
        scale = scale + jnp.where((lanes == s) & (rows_of == s), 1.0 / counts[s], 0.0)
    loss_ref[...] = jnp.sum(sums * scale, axis=0, keepdims=True)[:, 0:5]


def hand_on(losses_ref, grads_ref, loss_ref, grad_ref):
    loss_ref[...] = losses_ref[...]
    grad_ref[...] = grads_ref[...]


def on_device(*args):
    (real, fake, w1, w2, w3, w4, w5, *vectors) = args
    flat = [w.reshape(-1, w.shape[-1]) for w in (w2, w3, w4, w5)]
    vectors = [v.reshape(1, -1) for v in vectors]
    vmem = pl.BlockSpec(memory_space=pltpu.VMEM)
    anywhere = pl.BlockSpec(memory_space=pl.ANY)
    v = pltpu.VMEM
    dma = pltpu.SemaphoreType.DMA
    scratch = [v(a.shape, a.dtype) for a in (real, fake, w1, *vectors)] + [
        v((4, 256, 256), BF), v((256, 384), BF), v((1152, 256), BF), v((2304, 512), BF),
        v((4608, 512), BF), v((16, 512), F32), v((9, 256, 256), BF), v((8, 256), F32),
        v((4, 256, 256), BF),
        v((22, 256, 256), BF), v((10, 128, 384), BF), v((4, 64, 768), BF), v((10, 32, 1536), BF),
        v((12, 128, 384), BF), v((8, 64, 768), BF), v((6, 32, 1536), BF), v((12, 16, 1536), BF),
        v((512, 256), BF),
        v((9, 256, 256), BF), v((9, 128, 256), F32), v((6, 256, 256), BF),
        v((6, 128, 256), F32), v((4, 256, 256), BF), v((4, 128, 256), F32),
        v((9, 128, 256), F32), v((9, 128, 256), F32), v((6, 128, 256), F32),
        v((6, 128, 256), F32), v((8, 64, 256), F32), v((8, 64, 256), F32),
        v((2, 32, 512), F32), v((2, 32, 512), F32),
        v((96, 256), BF), v((2, 96, 256), BF), v((32, 512), BF), v((8, 32, 512), BF),
        v((4, 32, 512), BF), v((2, 4, 32, 512), BF),
        v((5, 8, 128), F32), v((3, 8, 128), F32), v((8, 8, 128), F32), v((8, 8, 128), F32),
        v((4, 8, 128), F32),
        dma((13,)), dma((9,)), dma((2, 2)), dma((2, 2)), dma((7,)), dma((7,)), dma((24,)), dma((24,)),
    ]
    losses, grads = pl.pallas_call(
        body,
        out_shape=(v((1, 5), F32), v((1, 3, 16, 256), F32)),
        in_specs=[anywhere] * 17,
        out_specs=(vmem, vmem),
        scratch_shapes=scratch,
        compiler_params=pltpu.CompilerParams(
            collective_id=0, has_side_effects=True, vmem_limit_bytes=56 << 20
        ),
        name="whole_step",
    )(real, fake, w1, *flat, *vectors)
    losses, grads = pl.pallas_call(
        hand_on,
        out_shape=(
            jax.ShapeDtypeStruct((1, 5), F32),
            jax.ShapeDtypeStruct((1, 3, 16, 256), F32),
        ),
        in_specs=[vmem] * 2,
        out_specs=(vmem, vmem),
        name="hand_on",
    )(
        pltpu.with_memory_space_constraint(losses, pltpu.VMEM),
        pltpu.with_memory_space_constraint(grads, pltpu.VMEM),
    )
    return (losses.reshape(5), grads)


def solution(mesh):
    frames = P("dp", None, "rows", None)
    return jax.shard_map(
        on_device,
        mesh=mesh,
        in_specs=(frames, frames) + (P(),) * 15,
        out_specs=(P(), frames),
        check_vma=False,
    )
```

```python
import functools

import jax
import jax.numpy as jnp
from jax import lax
from jax.experimental import pallas as pl
from jax.experimental.pallas import tpu as pltpu
from jax.sharding import PartitionSpec as P

MESH = pl.DeviceIdType.MESH
F32 = jnp.float32
BF = jnp.bfloat16
EPS = 1e-06
ROOT = 0.7978845608028654
CUBE = 0.044715

ROWS = 8
NZ = 8
NY = 4


def dot(a, b):
    return lax.dot_general(a, b, (((1,), (0,)), ((), ())), preferred_element_type=F32)


def dot_t(a, b):
    return lax.dot_general(a, b, (((1,), (1,)), ((), ())), preferred_element_type=F32)


def iota(shape, dim):
    return lax.broadcasted_iota(jnp.int32, shape, dim)


def onehot(cond):
    return jnp.where(cond, 1.0, 0.0).astype(BF)


def rounded(x):
    return x.astype(BF).astype(F32)


def gelu(h):
    t = jnp.tanh(h * (2.0 * ROOT + (8.0 * ROOT * CUBE) * (h * h)))
    return h + h * t


def gelu_both(h):
    h2 = h * h
    t = jnp.tanh(h * (2.0 * ROOT + (8.0 * ROOT * CUBE) * h2))
    ht = h * t
    slope = (0.5 + 0.5 * t) + (h - ht * t) * (ROOT + (12.0 * ROOT * CUBE) * h2)
    return h + ht, slope


def slope_of(h):
    h2 = h * h
    t = jnp.tanh(h * (2.0 * ROOT + (8.0 * ROOT * CUBE) * h2))
    return (0.5 + 0.5 * t) + (h - h * t * t) * (ROOT + (12.0 * ROOT * CUBE) * h2)


def tap(r, f, lin, total):
    a = lax.rsqrt(total(r * r) + EPS)
    b = lax.rsqrt(total(f * f) + EPS)
    nf = f * b
    d = r * a - nf
    ld = lin * d
    grad = (ld - nf * total(nf * ld)) * (-2.0 * b)
    return ld * d, grad


def lane_sum(x):
    return jnp.sum(x, axis=-1, keepdims=True)


def fold(x):
    m, c = x.shape
    y = jnp.sum(x.reshape(m // 8, 8, c), axis=0)
    out = y[:, 0:128]
    for j in range(1, c // 128):
        out = out + y[:, j * 128 : (j + 1) * 128]
    return out


def shifted(v, phases):
    c = v.shape[-1]
    q = iota((16, c), 0)
    n = phases * 16
    tail = jnp.where(q < 15, pltpu.roll(v[0:16], 15, 0), 0.0)
    head = jnp.where(q > 0, pltpu.roll(v[n - 16 : n], 1, 0), 0.0)
    if phases == 1:
        return head, tail
    left = jnp.concatenate([head, v[0 : n - 16]], axis=0)
    right = jnp.concatenate([v[16:n], tail], axis=0)
    return left, right


def pool_cols(v, phases):
    c = v.shape[-1]
    return jnp.sum(v.reshape(phases // 2, 2, 16, c), axis=1).reshape(phases * 8, c)


def spread_cols(v, phases):
    c = v.shape[-1]
    y = jnp.broadcast_to(v.reshape(phases, 1, 16, c), (phases, 2, 16, c))
    return y.reshape(phases * 32, c)


def body(
    real_hbm, fake_hbm, w1_hbm, w2_hbm, w3_hbm, w4_hbm, w5_hbm,
    b1_hbm, b2_hbm, b3_hbm, b4_hbm, b5_hbm, l1_hbm, l2_hbm, l3_hbm, l4_hbm, l5_hbm,
    loss_ref, grad_ref,
    real_ref, fake_ref, w1_ref,
    b1_ref, b2_ref, b3_ref, b4_ref, b5_ref, l1_ref, l2_ref, l3_ref, l4_ref, l5_ref,
    w2s, w2t, w3s, w4s, w5s, wsm, wb, vec, tt,
    x2, x3, x4, x5, g2, g3, g4, g5, back,
    act1, sl1, act2, sl2, act3, sl3,
    a1, s1, a2, s2, a3, s3, a4, s4,
    stage0, land0, stage5, land5, stage4, land4,
    parts, own, lrow, lz, ly,
    isem, wsem, ssem, rsem, gsend, grecv, lsend, lrecv,
):
    dp = lax.axis_index("dp")
    me = lax.axis_index("rows")
    zi = lax.rem(dp, NZ)
    yi = lax.div(dp, NZ)
    not_first = me > 0
    not_last = me < ROWS - 1

    def row_peer(k):
        return (dp, lax.rem(me + k, ROWS))

    def z_peer(k):
        return (yi * NZ + lax.rem(zi + k, NZ), me)

    def y_peer(k):
        return (lax.rem(yi + k, NY) * NZ + zi, me)

    barrier = pltpu.get_barrier_semaphore()
    peers = (
        [row_peer(k) for k in range(1, ROWS)]
        + [z_peer(k) for k in range(1, NZ)]
        + [y_peer(k) for k in range(1, NY)]
    )
    for peer in peers:
        pl.semaphore_signal(barrier, inc=1, device_id=peer, device_id_type=MESH)

    small_inputs = (
        (real_hbm, real_ref), (fake_hbm, fake_ref), (w1_hbm, w1_ref),
        (b1_hbm, b1_ref), (b2_hbm, b2_ref), (b3_hbm, b3_ref), (b4_hbm, b4_ref), (b5_hbm, b5_ref),
        (l1_hbm, l1_ref), (l2_hbm, l2_ref), (l3_hbm, l3_ref), (l4_hbm, l4_ref), (l5_hbm, l5_ref),
    )
    ci = [
        pltpu.make_async_copy(src, dst, isem.at[n]) for n, (src, dst) in enumerate(small_inputs)
    ]
    for c in ci:
        c.start()

    cw2 = [
        pltpu.make_async_copy(
            w2_hbm.at[pl.ds(ky * 192, 192)],
            w2s.at[ky + half, pl.ds(0, 192), pl.ds(half * 128, 128)],
            wsem.at[2 * ky + half],
        )
        for ky in range(3)
        for half in range(2)
    ]
    cw3 = pltpu.make_async_copy(w3_hbm, w3s, wsem.at[6])
    cw4 = pltpu.make_async_copy(w4_hbm, w4s, wsem.at[7])
    cw5 = pltpu.make_async_copy(w5_hbm, w5s, wsem.at[8])
    for c in cw2 + [cw3, cw4, cw5]:
        c.start()


    def beside(first, second, land, n):
        up = pltpu.make_async_remote_copy(
            src_ref=first, dst_ref=land.at[1], send_sem=ssem.at[n, 0],
            recv_sem=rsem.at[n, 1], device_id=row_peer(ROWS - 1), device_id_type=MESH,
        )
        down = pltpu.make_async_remote_copy(
            src_ref=second, dst_ref=land.at[0], send_sem=ssem.at[n, 1],
            recv_sem=rsem.at[n, 0], device_id=row_peer(1), device_id_type=MESH,
        )
        return up, down

    for c in ci:
        c.wait()
    stage0[0:48] = real_ref[0].reshape(48, 256)
    stage0[48:96] = fake_ref[0].reshape(48, 256)

    wsm[...] = jnp.zeros_like(wsm)
    for ky in range(3):
        for kx in range(3):
            piece = w1_ref[ky, kx].astype(F32) * 0.5
            for p in range(2):
                lane = (kx + p) * 128 + p * 64
                wsm[ky * 3 : ky * 3 + 3, lane : lane + 64] = piece
    small = wsm[...].astype(BF)

    for k in range(9):
        idx = iota((64, 16), 0)
        n = iota((64, 16), 1)
        ky = jnp.where(n >= 3, 1, 0) + jnp.where(n >= 6, 1, 0)
        ci = n - 3 * ky
        for half in range(2):
            row = 2 * k + half if k < 8 else 17 * half - 1
            at = row + ky - 1
            inner = (idx >> 4 == ci) & ((idx & 15) == at) & (idx < 48)
            above = (idx - 48 == ci) & (at == -1)
            below = (idx - 51 == ci) & (at == 16)
            block = dot(onehot((inner | above | below) & (n < 9)), small).astype(BF)
            for d in range(4):
                wb[k, d * 64 : (d + 1) * 64, half * 128 : (half + 1) * 128] = block[
                    :, d * 128 : (d + 1) * 128
                ]

    for row, ref, scale in ((0, b1_ref, 0.5), (1, l1_ref, 1.0)):
        for q in range(4):
            vec[row : row + 1, q * 64 : (q + 1) * 64] = ref[...] * scale
    for row, ref, scale in ((2, b2_ref, 0.5), (3, l2_ref, 1.0)):
        for q in range(2):
            vec[row : row + 1, q * 128 : (q + 1) * 128] = ref[...] * scale
    ones_part = onehot(iota((256, 256), 0) >> 6 == iota((256, 256), 1) >> 6)
    ones_rows = onehot(iota((256, 256), 0) >> 7 == iota((256, 256), 1) >> 7)

    def sum_part(x):
        return dot(x.astype(BF), ones_part)

    def sum_rows(x):
        return dot(x.astype(BF), ones_rows)

    parts[...] = jnp.zeros_like(parts)
    w2s[:, 192:256, :] = jnp.zeros((4, 64, 256), BF)
    w2s[0, 0:192, 128:256] = jnp.zeros((192, 128), BF)
    w2s[3, 0:192, 0:128] = jnp.zeros((192, 128), BF)

    pos = iota((128, 256), 0)
    col = iota((128, 256), 1)
    base = 16 * (pos & 15) + 2 * (pos >> 4)
    take = onehot(col == base)
    for d in range(4):
        back[d * 128 : (d + 1) * 128, :] = onehot(col == base + d - 1)

    def patches(slot, images, sources):
        for i in range(2):
            halo = jnp.zeros((16, 256), F32)
            for source, row, off, ok in sources:
                j = iota((16, 96), 0) - off
                k = iota((16, 96), 1)
                pick = (j >= 0) & (j < 3) & (k == i * 48 + j * 16 + row)
                if ok is not None:
                    pick = pick & ok
                halo = halo + dot(onehot(pick), source)
            whole = jnp.concatenate([images[i * 48 : (i + 1) * 48].astype(F32), halo], axis=0)
            cols = iota((64, 256), 1)
            turned = []
            for d in range(4):
                dx = d - 1
                moved = whole if dx == 0 else pltpu.roll(whole, (-dx) % 256, 1)
                moved = jnp.where((cols + dx >= 0) & (cols + dx < 256), moved, 0.0)
                turned.append(moved.astype(BF))
            tt[slot, i * 128 : (i + 1) * 128, :] = dot_t(
                take, jnp.concatenate(turned, axis=0)
            ).astype(BF)

    mine = stage0[...]
    patches(0, mine, ())

    pl.semaphore_wait(barrier, len(peers))
    c0 = beside(stage0, stage0, land0, 0)
    for c in c0:
        c.start()

    lane = iota((128, 128), 1)
    bias1 = vec[0:1, :]
    lin1 = vec[1:2, :]

    def put2(row, v):
        for i in range(2):
            w = v[i * 128 : (i + 1) * 128]
            left, right = shifted(w, 8)
            x2[row, i * 128 : (i + 1) * 128, 0:128] = jnp.where(lane < 64, left, w).astype(BF)
            x2[row, i * 128 : (i + 1) * 128, 128:256] = right.astype(BF)

    def segment1(slot, k, p, keep, ok):
        pre = dot(tt[slot], wb[k]) + bias1
        act = rounded(gelu(pre))
        if keep is not None:
            slope = pre[128:256]
            if keep == "left":
                act1[8, :, 0:128] = act[:, 128:256].astype(BF)
                sl1[8, :, 0:128] = slope[:, 128:256]
            elif keep == "right":
                act1[8, :, 128:256] = act[:, 0:128].astype(BF)
                sl1[8, :, 128:256] = slope[:, 0:128]
            else:
                act1[k] = act.astype(BF)
                sl1[k] = slope
        s = act[:, 0:128] + act[:, 128:256]
        v = rounded((s + pltpu.roll(s, 64, 1)) * 0.125)
        if ok is not None:
            v = jnp.where(ok, v, 0.0)
        put2(p, v)

    def tap1(k, counted):
        act = act1[k].astype(F32)
        terms, grad = tap(act[0:128], act[128:256], lin1, sum_part)
        if counted:
            parts[0] += fold(terms)
        slope = slope_of(sl1[k])
        a1[k] = slope * grad
        s1[k] = slope * 0.25

    for k in range(1, 7):
        segment1(0, k, 7 + k, "own", None)
    for k in range(1, 7):
        tap1(k, True)

    for c in cw2:
        c.wait()
    for at, ky in ((0, 0), (64, 2), (128, 1), (192, 1)):
        for kx in range(3):
            piece = w2s[ky, kx * 64 : (kx + 1) * 64, 0:128]
            w2t[at : at + 64, kx * 128 : (kx + 1) * 128] = piece

    def put(ref, row, v, phases, c):
        n = phases * 16
        for i in range(2):
            w = v[i * n : (i + 1) * n]
            left, right = shifted(w, phases)
            ref[row, i * n : (i + 1) * n, 0:c] = left.astype(BF)
            ref[row, i * n : (i + 1) * n, c : 2 * c] = w.astype(BF)
            ref[row, i * n : (i + 1) * n, 2 * c : 3 * c] = right.astype(BF)

    bias2 = vec[2:3, :]
    lin2 = vec[3:4, :]

    def segment2(m):
        pre = bias2
        for d in range(4):
            pre = pre + dot(x2[2 * m + d], w2s[d])
        act = rounded(gelu(pre))
        if 2 <= m < 8:
            act2[m - 2] = act.astype(BF)
            sl2[m - 2] = pre[128:256]
        v = rounded(pool_cols(act[:, 0:128] + act[:, 128:256], 16) * 0.125)
        if m < 3:
            v = jnp.where(not_first, v, 0.0)
        if m >= 7:
            v = jnp.where(not_last, v, 0.0)
        put(x3, m, v, 4, 128)

    segment2(4)
    segment2(5)
    for c in c0:
        c.wait()
    upper = land0[0]
    lower = land0[1]
    patches(1, mine, ((upper, 15, 0, not_first), (lower, 0, 3, not_last)))
    patches(2, upper, ((mine, 0, 3, None),))
    patches(3, lower, ((mine, 15, 0, None),))
    segment1(2, 7, 6, "left", not_first)
    segment1(1, 0, 7, "own", None)
    segment1(1, 7, 14, "own", None)
    segment1(3, 0, 15, "right", not_last)

    for k in range(1, 7):
        segment1(2, k, k - 1, None, not_first)
        segment1(3, k, 15 + k, None, not_last)

    for m in (0, 1, 2, 3, 6, 7, 8, 9):
        segment2(m)

    def both(pre, n):
        parts_of = []
        slopes = []
        for row in range(2):
            top = 2 * row * n
            parts_of.append(gelu(pre[top : top + n]))
            act, slope = gelu_both(pre[top + n : top + 2 * n])
            parts_of.append(act)
            slopes.append(slope)
        return rounded(jnp.concatenate(parts_of, axis=0)), jnp.concatenate(slopes, axis=0)

    cw3.wait()

    def segment3(n):
        rows = [x3[2 * n + ky : 2 * n + ky + 2].reshape(256, 384) for ky in range(3)]
        pre = dot(jnp.concatenate(rows, axis=1), w3s[...]) + b3_ref[...] * 0.5
        act = rounded(gelu(pre))
        act3[n] = act.astype(BF)
        sl3[n] = jnp.concatenate([pre[64:128], pre[192:256]], axis=0)
        v = rounded(pool_cols(act[0:128] + act[128:256], 8) * 0.125)
        if n < 1:
            v = jnp.where(not_first, v, 0.0)
        if n >= 3:
            v = jnp.where(not_last, v, 0.0)
        put(x4, n, v, 2, 256)

    for n in range(4):
        segment3(n)

    cw4.wait()
    pre = b4_ref[...] * 0.5
    for ky in range(3):
        rows = x4[ky : ky + 2].reshape(128, 768)
        pre = pre + dot(rows, w4s[ky * 768 : (ky + 1) * 768, :])
    act, slope = both(pre, 32)
    stage5[...] = (pool_cols(act[0:64] + act[64:128], 4) * 0.125).astype(BF)
    c5 = [
        pltpu.make_async_remote_copy(
            src_ref=stage5, dst_ref=land5.at[me], send_sem=gsend.at[k - 1],
            recv_sem=grecv.at[k - 1], device_id=row_peer(k), device_id_type=MESH,
        )
        for k in range(1, ROWS)
    ]
    for c in c5:
        c.start()
    land5[me] = stage5[...]

    act = act.reshape(2, 2, 32, 512)
    terms, grad = tap(
        act[:, 0].reshape(64, 512), act[:, 1].reshape(64, 512), l4_ref[...], lane_sum
    )
    parts[3] += fold(terms)
    a = slope * (64.0 * grad)
    s = slope * 0.25
    a4[...] = a.reshape(2, 32, 512)
    s4[...] = s.reshape(2, 32, 512)
    stage4[0:2] = a.astype(BF).reshape(2, 32, 512)
    stage4[2:4] = s.astype(BF).reshape(2, 32, 512)
    c4 = beside(stage4, stage4, land4, 1)
    for c in c4:
        c.start()

    def tap3(n, counted):
        act = act3[n].astype(F32).reshape(2, 2, 64, 256)
        slope = slope_of(sl3[n])
        terms, grad = tap(
            act[:, 0].reshape(128, 256), act[:, 1].reshape(128, 256), l3_ref[...], lane_sum
        )
        if counted:
            parts[2] += fold(terms)
        a3[2 * n : 2 * n + 2] = (slope * (16.0 * grad)).reshape(2, 64, 256)
        s3[2 * n : 2 * n + 2] = (slope * 0.25).reshape(2, 64, 256)

    def tap2(m, counted):
        act = act2[m - 2].astype(F32)
        slope = slope_of(sl2[m - 2])
        terms, grad = tap(act[0:128], act[128:256], lin2, sum_rows)
        if counted:
            parts[1] += fold(terms)
        a2[m - 2] = slope * (4.0 * grad)
        s2[m - 2] = slope * 0.25

    tap1(0, True)
    tap1(7, True)
    tap1(8, False)
    tap3(1, True)
    tap3(2, True)

    for m in range(3, 7):
        tap2(m, True)

    def spread_loss(src, land, slot, peer, count, first):
        copies = [
            pltpu.make_async_remote_copy(
                src_ref=src, dst_ref=land.at[slot], send_sem=lsend.at[first + k],
                recv_sem=lrecv.at[first + k], device_id=peer(k), device_id_type=MESH,
            )
            for k in range(1, count)
        ]
        for c in copies:
            c.start()
        land[slot] = src[...]
        return copies

    def gathered_loss(copies, land, count):
        for c in copies:
            c.wait()
        total = land[0]
        for j in range(1, count):
            total = total + land[j]
        return total

    rows_of = iota((8, 128), 0)
    sums = jnp.zeros((8, 128), F32)
    for s in range(4):
        sums = sums + jnp.where(rows_of == s, jnp.sum(parts[s], axis=0, keepdims=True), 0.0)
    own[0] = sums
    cl = spread_loss(own.at[0], lrow, me, row_peer, ROWS, 0)

    tap2(2, False)
    tap2(7, False)
    tap3(0, False)
    tap3(3, False)

    for row in (0, 9):
        x5[row] = jnp.zeros((32, 1536), BF)
    for row in (0, 1, 10, 11):
        g5[row] = jnp.zeros((16, 1536), BF)
    cw5.wait()
    for c in c5:
        c.wait()
    for row in range(ROWS):
        put(x5, row + 1, land5[row].astype(F32), 1, 512)
    pre = b5_ref[...] * 0.5
    for ky in range(3):
        rows = x5[ky : ky + 8].reshape(256, 1536)
        pre = pre + dot(rows, w5s[ky * 1536 : (ky + 1) * 1536, :])
    pre = pre.reshape(8, 2, 16, 512)
    act_r = rounded(gelu(pre[:, 0].reshape(128, 512)))
    act_f, slope = gelu_both(pre[:, 1].reshape(128, 512))
    act_f = rounded(act_f)
    terms, grad = tap(act_r, act_f, l5_ref[...], lane_sum)
    gpre = rounded(slope * (256.0 * grad))

    def put_back(ref, row, v, phases, c):
        left, right = shifted(v, phases)
        ref[row, :, 0:c] = right.astype(BF)
        ref[row, :, c : 2 * c] = v.astype(BF)
        ref[row, :, 2 * c : 3 * c] = left.astype(BF)

    for row in range(ROWS):
        put_back(g5, row + 2, gpre[row * 16 : (row + 1) * 16], 1, 512)
    fifth = jnp.sum(fold(terms), axis=0, keepdims=True)
    own[1] = gathered_loss(cl, lrow, ROWS) + jnp.where(rows_of == 4, fifth, 0.0)
    cl = spread_loss(own.at[1], lz, zi, z_peer, NZ, 8)

    gin = jnp.zeros((48, 512), F32)
    for ky in range(3):
        rows = g5[pl.ds(me + 2 - ky, 3)].reshape(48, 1536)
        for kx in range(3):
            n = (ky * 3 + kx) * 512
            gin = gin + dot_t(rows[:, kx * 512 : (kx + 1) * 512], w5s[n : n + 512, :])

    for c in c4:
        c.wait()
    for u in range(6):
        wide = spread_cols(gin[(u // 2) * 16 : (u // 2 + 1) * 16], 1)
        if 2 <= u < 4:
            v = a4[u - 2] + s4[u - 2] * wide
        else:
            side, j, ok = (0, u, not_first) if u < 2 else (1, u - 4, not_last)
            a = land4[side, j].astype(F32)
            s = land4[side, 2 + j].astype(F32)
            v = jnp.where(ok, a + s * wide, 0.0)
        put_back(g4, u, rounded(v), 2, 512)
    gin = jnp.zeros((128, 256), F32)
    for ky in range(3):
        rows = g4[2 - ky : 6 - ky].reshape(128, 1536)
        for kx in range(3):
            n = (ky * 3 + kx) * 256
            gin = gin + dot_t(rows[:, kx * 512 : (kx + 1) * 512], w4s[n : n + 256, :])

    for j in range(8):
        wide = spread_cols(gin[(j // 2) * 32 : (j // 2 + 1) * 32], 2)
        v = a3[j] + s3[j] * wide
        if j < 2:
            v = jnp.where(not_first, v, 0.0)
        if j >= 6:
            v = jnp.where(not_last, v, 0.0)
        put_back(g3, j, rounded(v), 4, 256)
    gin = 0.0
    for ky in range(3):
        rows = g3[2 - ky : 8 - ky].reshape(384, 768)
        for kx in range(3):
            n = (ky * 3 + kx) * 128
            gin = gin + dot_t(rows[:, kx * 256 : (kx + 1) * 256], w3s[n : n + 128, :])
    own[2] = gathered_loss(cl, lz, NZ)
    cl = spread_loss(own.at[2], ly, yi, y_peer, NY, 16)

    for j in range(12):
        wide = spread_cols(gin[(j // 2) * 64 : (j // 2 + 1) * 64], 4)
        at = (j % 2) * 128
        v = a2[j // 2, :, at : at + 128] + s2[j // 2, :, at : at + 128] * wide
        if j < 2:
            v = jnp.where(not_first, v, 0.0)
        if j >= 10:
            v = jnp.where(not_last, v, 0.0)
        put_back(g2, j, rounded(v), 8, 128)

    products = []
    for n in range(6):
        two = dot_t(g2[2 * n : 2 * n + 2].reshape(256, 384), w2t[...])
        products += [two[0:128], two[128:256]]

    def gin2(z):
        u = jnp.where(lane < 64, products[z + 2][:, 0:128], products[z][:, 0:128])
        return u + pltpu.roll(u, 64, 1) + products[z + 1][:, 128:256]

    across = jnp.zeros((256, 128), F32)
    for k in range(9):
        if k < 8:
            g = gin2(k + 1)
            wide = jnp.concatenate([g, g], axis=1)
            v = a1[k] + s1[k] * wide
        else:
            above = a1[8, :, 0:128] + s1[8, :, 0:128] * gin2(0)
            below = a1[8, :, 128:256] + s1[8, :, 128:256] * gin2(9)
            v = jnp.concatenate(
                [jnp.where(not_first, above, 0.0), jnp.where(not_last, below, 0.0)], axis=1
            )
        across = across + dot_t(wb[k], v.astype(BF))
    across = across * 2.0
    lined = jnp.concatenate([across[d * 64 : (d + 1) * 64] for d in range(4)], axis=1)
    high = lined.astype(BF)
    low = (lined - high.astype(F32)).astype(BF)
    out = dot(high, back[...]) + dot(low, back[...])
    grad_ref[0] = out[0:48].reshape(3, 16, 256)

    total = gathered_loss(cl, ly, NY)
    sums = jnp.sum(total, axis=1, keepdims=True)
    lanes = iota((8, 128), 1)
    counts = [32.0 * (128 >> s) * (256 >> s) for s in range(5)]
    scale = jnp.zeros((8, 128), F32)
    for s in range(5):
        scale = scale + jnp.where((lanes == s) & (rows_of == s), 1.0 / counts[s], 0.0)
    loss_ref[...] = jnp.sum(sums * scale, axis=0, keepdims=True)[:, 0:5]


def hand_on(losses_ref, grads_ref, loss_ref, grad_ref):
    loss_ref[...] = losses_ref[...]
    grad_ref[...] = grads_ref[...]


def on_device(*args):
    (real, fake, w1, w2, w3, w4, w5, *vectors) = args
    flat = [w.reshape(-1, w.shape[-1]) for w in (w2, w3, w4, w5)]
    vectors = [v.reshape(1, -1) for v in vectors]
    vmem = pl.BlockSpec(memory_space=pltpu.VMEM)
    anywhere = pl.BlockSpec(memory_space=pl.ANY)
    v = pltpu.VMEM
    dma = pltpu.SemaphoreType.DMA
    scratch = [v(a.shape, a.dtype) for a in (real, fake, w1, *vectors)] + [
        v((4, 256, 256), BF), v((256, 384), BF), v((1152, 256), BF), v((2304, 512), BF),
        v((4608, 512), BF), v((16, 512), F32), v((9, 256, 256), BF), v((8, 256), F32),
        v((4, 256, 256), BF),
        v((22, 256, 256), BF), v((10, 128, 384), BF), v((4, 64, 768), BF), v((10, 32, 1536), BF),
        v((12, 128, 384), BF), v((8, 64, 768), BF), v((6, 32, 1536), BF), v((12, 16, 1536), BF),
        v((512, 256), BF),
        v((9, 256, 256), BF), v((9, 128, 256), F32), v((6, 256, 256), BF),
        v((6, 128, 256), F32), v((4, 256, 256), BF), v((4, 128, 256), F32),
        v((9, 128, 256), F32), v((9, 128, 256), F32), v((6, 128, 256), F32),
        v((6, 128, 256), F32), v((8, 64, 256), F32), v((8, 64, 256), F32),
        v((2, 32, 512), F32), v((2, 32, 512), F32),
        v((96, 256), BF), v((2, 96, 256), BF), v((32, 512), BF), v((8, 32, 512), BF),
        v((4, 32, 512), BF), v((2, 4, 32, 512), BF),
        v((5, 8, 128), F32), v((3, 8, 128), F32), v((8, 8, 128), F32), v((8, 8, 128), F32),
        v((4, 8, 128), F32),
        dma((13,)), dma((9,)), dma((2, 2)), dma((2, 2)), dma((7,)), dma((7,)), dma((24,)), dma((24,)),
    ]
    losses, grads = pl.pallas_call(
        body,
        out_shape=(v((1, 5), F32), v((1, 3, 16, 256), F32)),
        in_specs=[anywhere] * 17,
        out_specs=(vmem, vmem),
        scratch_shapes=scratch,
        compiler_params=pltpu.CompilerParams(
            collective_id=0, has_side_effects=True, vmem_limit_bytes=56 << 20
        ),
        name="whole_step",
    )(real, fake, w1, *flat, *vectors)
    losses, grads = pl.pallas_call(
        hand_on,
        out_shape=(
            jax.ShapeDtypeStruct((1, 5), F32),
            jax.ShapeDtypeStruct((1, 3, 16, 256), F32),
        ),
        in_specs=[vmem] * 2,
        out_specs=(vmem, vmem),
        name="hand_on",
    )(
        pltpu.with_memory_space_constraint(losses, pltpu.VMEM),
        pltpu.with_memory_space_constraint(grads, pltpu.VMEM),
    )
    return (losses.reshape(5), grads)


def solution(mesh):
    frames = P("dp", None, "rows", None)
    return jax.shard_map(
        on_device,
        mesh=mesh,
        in_specs=(frames, frames) + (P(),) * 15,
        out_specs=(P(), frames),
        check_vma=False,
    )
```
